32 devices in a mesh: sec: 8 (over z, core), bond: 4 (over y, x).
Axes of the slice: x: 2, y: 2, z: 4, core: 2. Of those that a mesh axis runs over, the one named last changes fastest.
Arguments:
- left_env: bfloat16 [8, 512, 8, 512], P('sec', 'bond'), may hold values from -6 to 6
- site: bfloat16 [8, 512, 4, 512], P('sec', 'bond'), may hold values from -0.125 to 0.125
- psi: bfloat16 [8, 512, 4, 4, 512], P('sec', 'bond'), may hold values from -0.25 to 0.25
- right_env: bfloat16 [8, 8, 512, 512], P('sec'), may hold values from -0.09375 to 0.09375
- mpo: bfloat16 [8, 8, 4, 4], replicated, may hold values from -1 to 1
Outputs:
- new_left: bfloat16 [8, 512, 8, 512], P('sec', 'bond')
- product: bfloat16 [8, 512, 4, 4, 512], P('sec', 'bond')
The draws below stay inside these ranges and needn't reach their ends.
All inputs are finite; a program needn't handle non-finite values.
Results may differ from the reference program's by a relative error of at most 0.0095.
Values may be sent and summed in bfloat16 or wider, within the bound.
A program may use at most 128 MiB of HBM per device.

```python
import jax
import jax.numpy as jnp
from jax import lax

CHI = 512
MPO_W = 8
PHYS = 4
SECTIONS = 8


def level_of(stream_key, extent, cuts, low, high):
    factor_of = 1.0
    for dim, parts in cuts:
        heights = jax.random.uniform(jax.random.fold_in(jax.random.fold_in(stream_key, 6), dim), (parts,), jnp.float32, low / len(cuts), high / len(cuts))
        factor_of = factor_of * jnp.repeat(jnp.exp(heights), extent[dim] // parts).reshape((-1,) + (1,) * (len(extent) - 1 - dim))
    return factor_of


def gaussian(key, shape, spread, reach, pieces=(), held_as=jnp.bfloat16):
    drawn = jax.random.normal(key, shape, jnp.float32) * spread
    if len(pieces) > 0:
        drawn = level_of(key, shape, pieces, -0.22, 0.18) * drawn
    return jnp.clip(drawn, min=-reach, max=reach).astype(held_as)


def setup_inputs(seed: int = 0) -> dict:
    arg_keys = jax.random.split(jax.random.key(seed), 6)
    return {
        "left_env": gaussian(arg_keys[0], (SECTIONS, CHI, MPO_W, CHI), 1.0, 6.0, ((0, 8), (1, 4))),
        "site": gaussian(arg_keys[1], (SECTIONS, CHI, PHYS, CHI), (CHI * PHYS) ** -0.5, 0.125, ((0, 8), (1, 4))),
        "psi": gaussian(arg_keys[2], (SECTIONS, CHI, PHYS, PHYS, CHI), CHI ** -0.5, 0.25, ((0, 8), (1, 4))),
        "right_env": gaussian(arg_keys[3], (SECTIONS, MPO_W, CHI, CHI), (MPO_W * CHI) ** -0.5, 0.09375, ((0, 8),)),
        "mpo": gaussian(arg_keys[4], (MPO_W, MPO_W, PHYS, PHYS), (MPO_W * PHYS) ** -0.5, 1.0),
    }


def reference(left_env, site, psi, right_env, mpo):
    mpo_wide = mpo.astype(jnp.float32)

    def update(pair):
        left, tensor = pair
        first = jnp.dot(left.reshape(CHI * MPO_W, CHI), tensor.reshape(CHI, PHYS * CHI), preferred_element_type=jnp.float32)
        first = first.astype(jnp.bfloat16).reshape(CHI, MPO_W, PHYS, CHI)
        second = jnp.einsum("pmsb,mnsu->punb", first.astype(jnp.float32), mpo_wide).astype(jnp.bfloat16)
        fresh = jnp.dot(tensor.reshape(CHI * PHYS, CHI).T, second.reshape(CHI * PHYS, MPO_W * CHI), preferred_element_type=jnp.float32)
        return fresh.astype(jnp.bfloat16).reshape(CHI, MPO_W, CHI)

    new_left = lax.map(update, (left_env, site))
    two_site = jnp.einsum("mnsu,nkvw->msvuwk", mpo_wide, mpo_wide).astype(jnp.bfloat16).reshape(MPO_W * PHYS * PHYS, PHYS * PHYS * MPO_W)

    def apply(triple):
        left, pair, right = triple
        mixed = jnp.dot(left.reshape(CHI * MPO_W, CHI), pair.reshape(CHI, PHYS * PHYS * CHI), preferred_element_type=jnp.float32)
        mixed = mixed.astype(jnp.bfloat16).reshape(CHI, MPO_W * PHYS * PHYS, CHI)
        projected = jnp.einsum("pqc,qr->prc", mixed.astype(jnp.float32), two_site.astype(jnp.float32)).astype(jnp.bfloat16)
        result = jnp.dot(projected.reshape(CHI * PHYS * PHYS, MPO_W * CHI), right.reshape(MPO_W * CHI, CHI), preferred_element_type=jnp.float32)
        return result.astype(jnp.bfloat16).reshape(CHI, PHYS, PHYS, CHI)

    product = lax.map(apply, (jnp.roll(new_left, 1, axis=0), jnp.roll(psi, 1, axis=0), right_env))
    return new_left, product
```

```python
import functools

import jax
import jax.numpy as jnp
from jax import lax
from jax.experimental import pallas as pl
from jax.experimental.pallas import tpu as pltpu
from jax.sharding import PartitionSpec as P

MESH = pl.DeviceIdType.MESH
BF16 = jnp.bfloat16
F32 = jnp.float32


def mm(a, b):
    return jnp.dot(a, b, preferred_element_type=F32)


def kernel(
    dims,
    left_h, site_h, site_tr_h, psi_h, right_h, mix_h, pair_h,
    new_left, product,
    left, site, site_tr, mix, pair, right,
    second, part, rs1, send2, rs2, nl32, nl_in, psi, mixed, proj, acc,
    local_sem, send_sem, recv_sem,
):
    rows, width, phys, chi, group, cuts, batch = dims
    n_bond = 4
    pq = phys * phys
    step = chi // cuts
    sec = lax.axis_index("sec")
    me = lax.axis_index("bond")
    n_sec = lax.axis_size("sec")
    next_sec = lax.rem(sec + 1, n_sec)
    prev_sec = lax.rem(sec + n_sec - 1, n_sec)
    bx = (me // 2) * 2 + 1 - lax.rem(me, 2)
    by = lax.rem(me + 2, n_bond)
    bd = lax.rem(bx + 2, n_bond)
    to_x = {"bond": bx}
    to_y = {"bond": by}
    to_next = {"sec": next_sec}

    def block(owner):
        return pl.ds(pl.multiple_of(owner * rows, rows), rows)

    loads = {}
    for i, (name, src, dst) in enumerate((
        ("site", site_h, site.at[:, block(me), :]),
        ("left", left_h, left),
        ("mix", mix_h, mix),
        ("site_tr", site_tr_h, site_tr),
        ("pair", pair_h, pair),
        ("right", right_h, right),
    )):
        loads[name] = pltpu.make_async_copy(src, dst, local_sem.at[i])
        loads[name].start()

    barrier = pltpu.get_barrier_semaphore()
    for target in (to_x, to_y, to_next, {"sec": prev_sec}):
        pl.semaphore_signal(barrier, inc=1, device_id=target, device_id_type=MESH)
    pl.semaphore_wait(barrier, 4)

    started = []
    counter = {}

    def slot(key):
        return counter.setdefault(key, len(counter))

    def send(key, src, dst, target):
        i = slot(key)
        copy = pltpu.make_async_remote_copy(
            src_ref=src, dst_ref=dst, send_sem=send_sem.at[i], recv_sem=recv_sem.at[i],
            device_id=target, device_id_type=MESH,
        )
        copy.start()
        started.append(copy)

    def arrive(key, dst, target):
        i = slot(key)
        pltpu.make_async_remote_copy(
            src_ref=dst, dst_ref=dst, send_sem=send_sem.at[i], recv_sem=recv_sem.at[i],
            device_id=target, device_id_type=MESH,
        ).wait_recv()

    half_s = phys // 2
    send("site_x", site_h, site.at[:, block(me), :], to_x)
    send("site_y", site_h, site.at[:, block(me), :], to_y)

    chunks = [(cc, h) for cc in range(cuts) for h in range(2)]
    hp = pq // 2
    qp = hp // 2

    def region(q, owner, sub=None):
        cc, h = chunks[q]
        if sub is None:
            return psi.at[cc, pl.ds(h * hp, hp), block(owner), :]
        return psi.at[cc, pl.ds(h * hp + sub * qp, qp), block(owner), :]

    for q, (cc, h) in enumerate(chunks):
        send(("shift", q), psi_h.at[cc, pl.ds(h * hp, hp)], region(q, me), to_next)

    def spread(q):
        arrive(("shift", q), region(q, me), to_next)
        send(("psi_x", q), region(q, me), region(q, me), to_x)
        send(("psi_y", q), region(q, me), region(q, me), to_y)

    def relay(q):
        arrive(("psi_x", q), region(q, bx), to_x)
        send(("psi_xy", q), region(q, bx, 0), region(q, bx, 0), to_y)
        arrive(("psi_y", q), region(q, by), to_y)
        send(("psi_yx", q), region(q, by, 1), region(q, by, 1), to_x)

    def complete(q):
        arrive(("psi_xy", q), region(q, bd, 0), to_y)
        arrive(("psi_yx", q), region(q, bd, 1), to_x)

    lo, hi = pl.ds(0, half_s), pl.ds(half_s, phys - half_s)
    arrive("site_x", site.at[:, block(bx), :], to_x)
    send("site_xy", site.at[lo, block(bx), :], site.at[lo, block(bx), :], to_y)
    arrive("site_y", site.at[:, block(by), :], to_y)
    send("site_yx", site.at[hi, block(by), :], site.at[hi, block(by), :], to_x)
    spread(0)
    loads["site"].wait()
    loads["left"].wait()
    loads["mix"].wait()
    loads["site_tr"].wait()
    arrive("site_xy", site.at[lo, block(bd), :], to_y)
    arrive("site_yx", site.at[hi, block(bd), :], to_x)

    strip = group * width

    @pl.loop(0, rows // group)
    def _(g):
        ours = left[pl.ds(pl.multiple_of(g * strip, strip), strip), :]
        first = jnp.concatenate([mm(ours, site[s]).astype(BF16) for s in range(phys)], axis=0)
        out = mm(mix[...], first).astype(BF16)
        for u in range(phys):
            for n in range(width):
                at = (u * width + n) * group
                where = pl.multiple_of(u * rows + g * group, group)
                second[n, pl.ds(where, group), :] = out[at:at + group, :]

    relay(0)
    half_w = width // 2
    order = [k + d * half_w for k in range(half_w) for d in range(2)]

    def first_round(n):
        if n < half_w:
            send(("rs_own", n), part.at[n, block(bx), :], rs1.at[n, 0], to_x)
            send(("rs_far", n), part.at[n, block(bd), :], rs1.at[n, 1], to_x)
        else:
            send(("rs_own", n), part.at[n, block(by), :], rs1.at[n, 0], to_y)
            send(("rs_far", n), part.at[n, block(bd), :], rs1.at[n, 1], to_y)

    behind = None
    for n in order:
        part[n] = mm(site_tr[...], second[n]).astype(BF16)
        if behind is not None:
            first_round(behind)
        behind = n
    first_round(behind)
    spread(1)

    def second_round(n):
        if n < half_w:
            send(("rs_last", n), send2.at[n], rs2.at[n], to_y)
        else:
            send(("rs_last", n), send2.at[n], rs2.at[n], to_x)

    behind = None
    for n in order:
        src, other = (to_x, by) if n < half_w else (to_y, bx)
        arrive(("rs_far", n), rs1.at[n, 1], src)
        send2[n] = (part[n, block(other), :].astype(F32) + rs1[n, 1].astype(F32)).astype(BF16)
        if behind is not None:
            second_round(behind)
        behind = n
    second_round(behind)
    relay(1)
    spread(2)
    for n in order:
        src, last = (to_x, to_y) if n < half_w else (to_y, to_x)
        arrive(("rs_own", n), rs1.at[n, 0], src)
        arrive(("rs_last", n), rs2.at[n], last)
        total = part[n, block(me), :].astype(F32) + rs1[n, 0].astype(F32) + rs2[n].astype(F32)
        for i in range(chi // 128):
            nl32[i, pl.ds(n, rows, stride=width), :] = total[:, i * 128:(i + 1) * 128]
    for i in range(chi // 128):
        new_left[:, i * 128:(i + 1) * 128] = nl32[i].astype(BF16)
    send("left", new_left, nl_in, to_next)
    relay(2)
    spread(3)
    complete(0)
    complete(1)
    loads["pair"].wait()
    loads["right"].wait()
    arrive("left", nl_in, to_next)

    for cc in range(cuts):
        if cc == 1:
            complete(2)
            complete(3)

        @pl.loop(0, rows // batch)
        def _(g):
            tall = batch * width
            ours = nl_in[pl.ds(pl.multiple_of(g * tall, tall), tall), :]

            @pl.loop(0, pq)
            def _(s):
                mixed[s] = mm(ours, psi[cc, s])

            @pl.loop(0, batch, unroll=4)
            def _(p):
                here = mixed[:, pl.ds(pl.multiple_of(p * width, width), width), :]
                out = mm(pair[...], here.reshape(pq * width, step).astype(BF16)).astype(BF16)
                for k in range(width):
                    proj[k, pl.ds(pl.multiple_of(p * pq, pq), pq), :] = out[k * pq:(k + 1) * pq, :]

            total = mm(proj[0], right[0, pl.ds(cc * step, step), :])
            for k in range(1, width):
                total += mm(proj[k], right[k, pl.ds(cc * step, step), :])
            long = pl.ds(pl.multiple_of(g * batch * pq, batch * pq), batch * pq)
            if cc > 0:
                total += acc[long, :]
            if cc < cuts - 1:
                acc[long, :] = total
            else:
                product[long, :] = total.astype(BF16)

        if cc == 0:
            relay(3)

    for copy in started:
        copy.wait_send()


def fused(left_env, site, psi, right_env, mpo):
    _, rows, width, chi = left_env.shape
    phys = site.shape[2]
    pq = phys * phys
    group, cuts, batch = 16, 2, 32
    step = chi // cuts
    by_phys = site[0].transpose(1, 0, 2)
    site_tr = by_phys.reshape(phys * rows, chi).T
    pairs = psi[0].reshape(rows, pq, cuts, step).transpose(2, 1, 0, 3)
    eye = jnp.eye(group, dtype=BF16)
    mix = (
        mpo.transpose(3, 1, 2, 0)[:, :, None, :, None, :] * eye[None, None, :, None, :, None]
    ).reshape(phys * width * group, phys * group * width)
    pair = jnp.einsum("mnsu,nkvw->kuwsvm", mpo, mpo, preferred_element_type=F32)
    pair = pair.astype(BF16).reshape(width * pq, pq * width)
    n_sems = 80
    any_spec = pl.BlockSpec(memory_space=pl.ANY)
    vmem = pl.BlockSpec(memory_space=pltpu.VMEM)
    new_left, product = pl.pallas_call(
        functools.partial(kernel, (rows, width, phys, chi, group, cuts, batch)),
        out_shape=(
            jax.ShapeDtypeStruct((rows * width, chi), BF16),
            jax.ShapeDtypeStruct((rows * pq, chi), BF16),
        ),
        in_specs=[any_spec] * 7,
        out_specs=(vmem, vmem),
        scratch_shapes=[
            pltpu.VMEM((rows * width, chi), BF16),
            pltpu.VMEM((phys, chi, chi), BF16),
            pltpu.VMEM((chi, phys * rows), BF16),
            pltpu.VMEM(mix.shape, BF16),
            pltpu.VMEM(pair.shape, BF16),
            pltpu.VMEM((width, chi, chi), BF16),
            pltpu.VMEM((width, phys * rows, chi), BF16),
            pltpu.VMEM((width, chi, chi), BF16),
            pltpu.VMEM((width, 2, rows, chi), BF16),
            pltpu.VMEM((width, rows, chi), BF16),
            pltpu.VMEM((width, rows, chi), BF16),
            pltpu.VMEM((chi // 128, rows * width, 128), F32),
            pltpu.VMEM((rows * width, chi), BF16),
            pltpu.VMEM((cuts, pq, chi, step), BF16),
            pltpu.VMEM((pq, batch * width, step), F32),
            pltpu.VMEM((width, batch * pq, step), BF16),
            pltpu.VMEM((rows * pq, chi), F32),
            pltpu.SemaphoreType.DMA((6,)),
            pltpu.SemaphoreType.DMA((n_sems,)),
            pltpu.SemaphoreType.DMA((n_sems,)),
        ],
        compiler_params=pltpu.CompilerParams(
            collective_id=0, has_side_effects=True, vmem_limit_bytes=62 * 1024 * 1024
        ),
    )(left_env[0].reshape(rows * width, chi), by_phys, site_tr, pairs, right_env[0], mix, pair)
    return (
        new_left.reshape(1, rows, width, chi),
        product.reshape(1, rows, phys, phys, chi),
    )


def shifted(block, axis, distance):
    devices = range(lax.axis_size(axis))
    route = [((i - distance) % len(devices), i) for i in devices]
    return lax.ppermute(block, axis, route)


def shards(left_env, site, psi, right_env, mpo):
    left = left_env[0]
    tensor = site[0]
    rows = tensor.shape[0]
    phys = tensor.shape[1]
    chi = tensor.shape[2]
    width = left.shape[1]
    pair_source = shifted(psi[0], "sec", 1)
    offset = lax.axis_index("bond") * rows
    whole_left, whole_site = (
        lax.all_gather(left, "bond", axis=0, tiled=True),
        lax.all_gather(tensor, "bond", axis=0, tiled=True),
    )
    own_cols = lax.dynamic_slice_in_dim(whole_site, offset, rows, 2)
    first = jnp.dot(
        whole_left.reshape(chi * width, chi),
        own_cols.reshape(chi, phys * rows),
        preferred_element_type=jnp.float32,
    )
    first = first.astype(jnp.bfloat16).reshape(chi, width, phys, rows)
    second = jnp.einsum("pmsb,mnsu->punb", first, mpo, preferred_element_type=jnp.float32).astype(
        jnp.bfloat16
    )
    fresh = lax.dot_general(
        whole_site.reshape(chi * phys, chi),
        second.reshape(chi * phys, width * rows),
        (((0,), (0,)), ((), ())),
        preferred_element_type=jnp.float32,
    )
    fresh = fresh.astype(jnp.bfloat16).reshape(chi, width, rows)
    new_left = lax.all_to_all(fresh, "bond", split_axis=0, concat_axis=2, tiled=True)
    left_source = shifted(new_left, "sec", 1)
    source_flat = left_source.reshape(rows * width, chi)
    pair = pair_source.reshape(rows, phys * phys * chi)
    mixed = jnp.dot(
        source_flat,
        lax.all_gather(pair, "bond", axis=0, tiled=True),
        preferred_element_type=jnp.float32,
    )
    mixed = mixed.astype(jnp.bfloat16).reshape(rows, width * phys * phys, chi)
    two_site = jnp.einsum("mnsu,nkvw->msvuwk", mpo, mpo, preferred_element_type=jnp.float32)
    two_site = two_site.astype(jnp.bfloat16).reshape(width * phys * phys, phys * phys * width)
    projected = jnp.einsum(
        "pqc,qr->prc", mixed, two_site, preferred_element_type=jnp.float32
    ).astype(jnp.bfloat16)
    env_right = right_env[0].reshape(width * chi, chi)
    result = jnp.dot(
        projected.reshape(rows * phys * phys, width * chi),
        env_right,
        preferred_element_type=jnp.float32,
    ).astype(jnp.bfloat16)
    return (new_left[None], result.reshape(1, rows, phys, phys, chi))


def solution(mesh):
    in_specs = (
        P("sec", "bond", None, None),
        P("sec", "bond", None, None),
        P("sec", "bond", None, None, None),
        P("sec", None, None, None),
        P(),
    )
    out_specs = (P("sec", "bond", None, None), P("sec", "bond", None, None, None))
    body = fused if mesh.shape["bond"] == 4 else shards
    return jax.shard_map(body, mesh=mesh, in_specs=in_specs, out_specs=out_specs, check_vma=False)
```

```python
import functools

import jax
import jax.numpy as jnp
from jax import lax
from jax.experimental import pallas as pl
from jax.experimental.pallas import tpu as pltpu
from jax.sharding import PartitionSpec as P

MESH = pl.DeviceIdType.MESH
BF16 = jnp.bfloat16
F32 = jnp.float32


def mm(a, b):
    return jnp.dot(a, b, preferred_element_type=F32)


def kernel(
    dims,
    left_h, site_h, psi_h, right_h, mpo_h,
    new_left, product,
    left, site_raw, psi_raw, mpo, right,
    site_own, psi_own, site, site_tr, mix, pair,
    second, part, rs1, send2, rs2, nl_own, nl_in, psi, mixed, proj, acc,
    local_sem, send_sem, recv_sem,
):
    rows, width, phys, chi, group, cuts, batch = dims
    n_bond = 4
    pq = phys * phys
    sec = lax.axis_index("sec")
    me = lax.axis_index("bond")
    n_sec = lax.axis_size("sec")
    next_sec = lax.rem(sec + 1, n_sec)
    prev_sec = lax.rem(sec + n_sec - 1, n_sec)
    bx = (me // 2) * 2 + 1 - lax.rem(me, 2)
    by = lax.rem(me + 2, n_bond)
    bd = lax.rem(bx + 2, n_bond)
    to_x = {"bond": bx}
    to_y = {"bond": by}
    to_next = {"sec": next_sec}

    def block(owner):
        return pl.ds(pl.multiple_of(owner * rows, rows), rows)

    loads = {}
    for i, (name, src, dst) in enumerate((
        ("site", site_h, site_raw),
        ("psi", psi_h, psi_raw),
        ("mpo", mpo_h, mpo),
        ("left", left_h, left),
        ("right", right_h, right),
    )):
        loads[name] = pltpu.make_async_copy(src, dst, local_sem.at[i])
        loads[name].start()

    barrier = pltpu.get_barrier_semaphore()
    for target in (to_x, to_y, to_next, {"sec": prev_sec}):
        pl.semaphore_signal(barrier, inc=1, device_id=target, device_id_type=MESH)
    pl.semaphore_wait(barrier, 4)

    started = []
    counter = {}

    def slot(key):
        return counter.setdefault(key, len(counter))

    def send(key, src, dst, target):
        i = slot(key)
        copy = pltpu.make_async_remote_copy(
            src_ref=src, dst_ref=dst, send_sem=send_sem.at[i], recv_sem=recv_sem.at[i],
            device_id=target, device_id_type=MESH,
        )
        copy.start()
        started.append(copy)

    def arrive(key, dst, target):
        i = slot(key)
        pltpu.make_async_remote_copy(
            src_ref=dst, dst_ref=dst, send_sem=send_sem.at[i], recv_sem=recv_sem.at[i],
            device_id=target, device_id_type=MESH,
        ).wait_recv()

    lanes = chi // cuts

    loads["site"].wait()
    flat = site_raw[...].astype(F32).reshape(rows * phys, chi)
    for i in range(cuts):
        acc[i, :rows * phys, :] = flat[:, i * lanes:(i + 1) * lanes]
    for t in range(phys):
        for i in range(cuts):
            tile = acc[i, pl.ds(t, rows, stride=phys), :]
            site_own[t, :, i * lanes:(i + 1) * lanes] = tile.astype(BF16)
            site_tr[i * lanes:(i + 1) * lanes, t * rows:(t + 1) * rows] = tile.T.astype(BF16)
    site_here = pltpu.make_async_copy(site_own, site.at[:, block(me), :], local_sem.at[5])
    site_here.start()
    send("site_x", site_own, site.at[:, block(me), :], to_x)
    send("site_y", site_own, site.at[:, block(me), :], to_y)

    loads["psi"].wait()
    tall = 8

    @pl.loop(0, rows // tall)
    def _(g):
        flat = psi_raw[pl.ds(pl.multiple_of(g * tall, tall), tall)].astype(F32)
        flat = flat.reshape(tall * pq, chi)
        where = pl.ds(pl.multiple_of(g * tall * pq, tall * pq), tall * pq)
        for i in range(cuts):
            acc[i, where, :] = flat[:, i * lanes:(i + 1) * lanes]

    half = pq // 4

    def region(q, owner, sub=None):
        if sub is None:
            return psi.at[q, :, block(owner), :]
        return psi.at[q, pl.ds(sub * half, half), block(owner), :]

    for q in range(cuts):
        for t in range(pq):
            at = (t % 2) * lanes
            tile = acc[q, pl.ds(t, rows, stride=pq), :]
            psi_own[q, t // 2, :, at:at + lanes] = tile.astype(BF16)
        if q > 0:
            send(("shift", q - 1), psi_own.at[q - 1], region(q - 1, me), to_next)
    send(("shift", cuts - 1), psi_own.at[cuts - 1], region(cuts - 1, me), to_next)

    def spread(q):
        arrive(("shift", q), region(q, me), to_next)
        send(("psi_x", q), region(q, me), region(q, me), to_x)
        send(("psi_y", q), region(q, me), region(q, me), to_y)

    def relay(q):
        arrive(("psi_x", q), region(q, bx), to_x)
        send(("psi_xy", q), region(q, bx, 0), region(q, bx, 0), to_y)
        arrive(("psi_y", q), region(q, by), to_y)
        send(("psi_yx", q), region(q, by, 1), region(q, by, 1), to_x)

    def complete(q):
        arrive(("psi_xy", q), region(q, bd, 0), to_y)
        arrive(("psi_yx", q), region(q, bd, 1), to_x)

    loads["mpo"].wait()

    def iota(shape, axis):
        return lax.broadcasted_iota(jnp.int32, shape, axis)

    def one_hot(condition):
        return jnp.where(condition, 1.0, 0.0).astype(BF16)

    small = phys * width
    big = small * group
    tall_code = lax.div(iota((big, small), 0), group)
    spread_rows = one_hot(tall_code == iota((big, small), 1))
    col = iota((small, big), 1)
    col_code = lax.div(col, group * width) * width + lax.rem(col, width)
    spread_cols = one_hot(col_code == iota((small, big), 0))
    wide = mm(mm(spread_rows, mpo[...]).astype(BF16), spread_cols)
    same = lax.rem(iota((big, big), 0), group) == lax.rem(lax.div(iota((big, big), 1), width), group)
    mix[...] = jnp.where(same, wide, 0.0).astype(BF16)

    side = width * pq
    col = iota((small, side), 1)
    col_m = lax.rem(col, width)
    col_sv = lax.rem(lax.div(col, width), pq // 2) * 2 + lax.div(col, width * (pq // 2))
    col_s, col_v = lax.div(col_sv, phys), lax.rem(col_sv, phys)
    row = iota((side, small), 0)
    row_k, row_u, row_w = lax.div(row, pq), lax.rem(lax.div(row, phys), phys), lax.rem(row, phys)
    code_c, code_r = iota((small, side), 0), iota((side, small), 1)
    t1 = mm(mpo[...], one_hot(col_s * width + col_m == code_c)).astype(BF16)
    t2 = mm(one_hot(row_w * width + row_k == code_r), mpo[...]).astype(BF16)
    both = jnp.zeros((side, side), F32)
    for n in range(width):
        near = mm(one_hot(row_u * width + n == code_r), t1)
        both += near * mm(t2, one_hot(col_v * width + n == code_c))
    pair[...] = both.astype(BF16)

    cut_s = phys // 2
    lo, hi = pl.ds(0, cut_s), pl.ds(cut_s, phys - cut_s)
    arrive("site_x", site.at[:, block(bx), :], to_x)
    send("site_xy", site.at[lo, block(bx), :], site.at[lo, block(bx), :], to_y)
    arrive("site_y", site.at[:, block(by), :], to_y)
    send("site_yx", site.at[hi, block(by), :], site.at[hi, block(by), :], to_x)
    spread(0)
    loads["left"].wait()
    site_here.wait()
    arrive("site_xy", site.at[lo, block(bd), :], to_y)
    arrive("site_yx", site.at[hi, block(bd), :], to_x)

    strip = group * width

    @pl.loop(0, rows // group)
    def _(g):
        ours = left[pl.ds(pl.multiple_of(g * group, group), group)].astype(F32)
        ours = ours.reshape(strip, chi).astype(BF16)
        first = jnp.concatenate([mm(ours, site[s]).astype(BF16) for s in range(phys)], axis=0)
        out = mm(mix[...], first).astype(BF16)
        for u in range(phys):
            for n in range(width):
                at = (u * width + n) * group
                where = pl.multiple_of(u * rows + g * group, group)
                second[n, pl.ds(where, group), :] = out[at:at + group, :]

    relay(0)
    half_w = width // 2
    order = [k + d * half_w for k in range(half_w) for d in range(2)]

    def first_round(n):
        if n < half_w:
            send(("rs_own", n), part.at[n, block(bx), :], rs1.at[n, 0], to_x)
            send(("rs_far", n), part.at[n, block(bd), :], rs1.at[n, 1], to_x)
        else:
            send(("rs_own", n), part.at[n, block(by), :], rs1.at[n, 0], to_y)
            send(("rs_far", n), part.at[n, block(bd), :], rs1.at[n, 1], to_y)

    behind = None
    for n in order:
        part[n] = mm(site_tr[...], second[n]).astype(BF16)
        if behind is not None:
            first_round(behind)
        behind = n
    first_round(behind)
    spread(1)

    def second_round(n):
        if n < half_w:
            send(("rs_last", n), send2.at[n], rs2.at[n], to_y)
        else:
            send(("rs_last", n), send2.at[n], rs2.at[n], to_x)

    behind = None
    for n in order:
        src, other = (to_x, by) if n < half_w else (to_y, bx)
        arrive(("rs_far", n), rs1.at[n, 1], src)
        send2[n] = (part[n, block(other), :].astype(F32) + rs1[n, 1].astype(F32)).astype(BF16)
        if behind is not None:
            second_round(behind)
        behind = n
    second_round(behind)
    relay(1)
    spread(2)
    for n in order:
        src, last = (to_x, to_y) if n < half_w else (to_y, to_x)
        arrive(("rs_own", n), rs1.at[n, 0], src)
        arrive(("rs_last", n), rs2.at[n], last)
        total = part[n, block(me), :].astype(F32) + rs1[n, 0].astype(F32) + rs2[n].astype(F32)
        for i in range(cuts):
            acc[i, pl.ds(n, rows, stride=width), :] = total[:, i * lanes:(i + 1) * lanes]
    whole = jnp.concatenate([acc[i, :rows * width, :] for i in range(cuts)], axis=1)
    nl_own[...] = whole.astype(BF16)
    new_left[...] = whole.reshape(rows, width, chi).astype(BF16)
    send("left", nl_own, nl_in, to_next)
    relay(2)
    spread(3)
    loads["right"].wait()
    arrive("left", nl_in, to_next)

    for q in range(cuts):
        complete(q)

        @pl.loop(0, rows // batch)
        def _(g):
            high = batch * width
            ours = nl_in[pl.ds(pl.multiple_of(g * high, high), high), :]

            @pl.loop(0, pq // 2)
            def _(t):
                mixed[t] = mm(ours, psi[q, t])

            @pl.loop(0, batch // 2, unroll=4)
            def _(p):
                here = mixed[:, pl.ds(pl.multiple_of(p * 2 * width, 2 * width), 2 * width), :]
                tiles = []
                for i in range(2):
                    one = here[:, i * width:(i + 1) * width, :].reshape(pq // 2 * width, 2 * lanes)
                    tiles.append(jnp.concatenate([one[:, :lanes], one[:, lanes:]], axis=0))
                both = jnp.concatenate(tiles, axis=1).astype(BF16)
                out = mm(pair[...], both).astype(BF16)
                for i in range(2):
                    where = pl.ds(pl.multiple_of((p * 2 + i) * pq, pq), pq)
                    for k in range(width):
                        piece = out[k * pq:(k + 1) * pq, i * lanes:(i + 1) * lanes]
                        proj[where, k * lanes:(k + 1) * lanes] = piece

            env = right[:, q * lanes:(q + 1) * lanes, :].reshape(width * lanes, chi)
            total = mm(proj[...], env)
            long = pl.ds(pl.multiple_of(g * batch * pq, batch * pq), batch * pq)
            if q > 0:
                total += jnp.concatenate([acc[i, long, :] for i in range(cuts)], axis=1)
            if q < cuts - 1:
                for i in range(cuts):
                    acc[i, long, :] = total[:, i * lanes:(i + 1) * lanes]
            else:
                out = total.reshape(batch, phys, phys, chi).astype(BF16)
                product[pl.ds(pl.multiple_of(g * batch, batch), batch)] = out

        if q == 1:
            relay(3)

    for copy in started:
        copy.wait_send()


def fused(left_env, site, psi, right_env, mpo):
    _, rows, width, chi = left_env.shape
    phys = site.shape[2]
    pq = phys * phys
    group, cuts, batch = 16, 4, 64
    lanes = chi // cuts
    small = phys * width
    table = mpo.transpose(3, 1, 2, 0).reshape(small, small)
    n_sems = 80
    any_spec = pl.BlockSpec(memory_space=pl.ANY)
    vmem = pl.BlockSpec(memory_space=pltpu.VMEM)
    new_left, product = pl.pallas_call(
        functools.partial(kernel, (rows, width, phys, chi, group, cuts, batch)),
        out_shape=(
            jax.ShapeDtypeStruct((rows, width, chi), BF16),
            jax.ShapeDtypeStruct((rows, phys, phys, chi), BF16),
        ),
        in_specs=[any_spec] * 5,
        out_specs=(vmem, vmem),
        scratch_shapes=[
            pltpu.VMEM((rows, width, chi), BF16),
            pltpu.VMEM((rows, phys, chi), BF16),
            pltpu.VMEM((rows, phys, phys, chi), BF16),
            pltpu.VMEM((small, small), BF16),
            pltpu.VMEM((width, chi, chi), BF16),
            pltpu.VMEM((phys, rows, chi), BF16),
            pltpu.VMEM((cuts, pq // 2, rows, 2 * lanes), BF16),
            pltpu.VMEM((phys, chi, chi), BF16),
            pltpu.VMEM((chi, phys * rows), BF16),
            pltpu.VMEM((small * group, small * group), BF16),
            pltpu.VMEM((width * pq, width * pq), BF16),
            pltpu.VMEM((width, phys * rows, chi), BF16),
            pltpu.VMEM((width, chi, chi), BF16),
            pltpu.VMEM((width, 2, rows, chi), BF16),
            pltpu.VMEM((width, rows, chi), BF16),
            pltpu.VMEM((width, rows, chi), BF16),
            pltpu.VMEM((rows * width, chi), BF16),
            pltpu.VMEM((rows * width, chi), BF16),
            pltpu.VMEM((cuts, pq // 2, chi, 2 * lanes), BF16),
            pltpu.VMEM((pq // 2, batch * width, 2 * lanes), F32),
            pltpu.VMEM((batch * pq, width * lanes), BF16),
            pltpu.VMEM((cuts, rows * pq, lanes), F32),
            pltpu.SemaphoreType.DMA((6,)),
            pltpu.SemaphoreType.DMA((n_sems,)),
            pltpu.SemaphoreType.DMA((n_sems,)),
        ],
        compiler_params=pltpu.CompilerParams(
            collective_id=0, has_side_effects=True, vmem_limit_bytes=62 * 1024 * 1024
        ),
    )(left_env[0], site[0], psi[0], right_env[0], table)
    return new_left[None], product[None]


def shifted(block, axis, distance):
    devices = range(lax.axis_size(axis))
    route = [((i - distance) % len(devices), i) for i in devices]
    return lax.ppermute(block, axis, route)


def shards(left_env, site, psi, right_env, mpo):
    left = left_env[0]
    tensor = site[0]
    rows = tensor.shape[0]
    phys = tensor.shape[1]
    chi = tensor.shape[2]
    width = left.shape[1]
    pair_source = shifted(psi[0], "sec", 1)
    offset = lax.axis_index("bond") * rows
    whole_left, whole_site = (
        lax.all_gather(left, "bond", axis=0, tiled=True),
        lax.all_gather(tensor, "bond", axis=0, tiled=True),
    )
    own_cols = lax.dynamic_slice_in_dim(whole_site, offset, rows, 2)
    first = jnp.dot(
        whole_left.reshape(chi * width, chi),
        own_cols.reshape(chi, phys * rows),
        preferred_element_type=jnp.float32,
    )
    first = first.astype(jnp.bfloat16).reshape(chi, width, phys, rows)
    second = jnp.einsum("pmsb,mnsu->punb", first, mpo, preferred_element_type=jnp.float32).astype(
        jnp.bfloat16
    )
    fresh = lax.dot_general(
        whole_site.reshape(chi * phys, chi),
        second.reshape(chi * phys, width * rows),
        (((0,), (0,)), ((), ())),
        preferred_element_type=jnp.float32,
    )
    fresh = fresh.astype(jnp.bfloat16).reshape(chi, width, rows)
    new_left = lax.all_to_all(fresh, "bond", split_axis=0, concat_axis=2, tiled=True)
    left_source = shifted(new_left, "sec", 1)
    source_flat = left_source.reshape(rows * width, chi)
    pair = pair_source.reshape(rows, phys * phys * chi)
    mixed = jnp.dot(
        source_flat,
        lax.all_gather(pair, "bond", axis=0, tiled=True),
        preferred_element_type=jnp.float32,
    )
    mixed = mixed.astype(jnp.bfloat16).reshape(rows, width * phys * phys, chi)
    two_site = jnp.einsum("mnsu,nkvw->msvuwk", mpo, mpo, preferred_element_type=jnp.float32)
    two_site = two_site.astype(jnp.bfloat16).reshape(width * phys * phys, phys * phys * width)
    projected = jnp.einsum(
        "pqc,qr->prc", mixed, two_site, preferred_element_type=jnp.float32
    ).astype(jnp.bfloat16)
    env_right = right_env[0].reshape(width * chi, chi)
    result = jnp.dot(
        projected.reshape(rows * phys * phys, width * chi),
        env_right,
        preferred_element_type=jnp.float32,
    ).astype(jnp.bfloat16)
    return (new_left[None], result.reshape(1, rows, phys, phys, chi))


def solution(mesh):
    in_specs = (
        P("sec", "bond", None, None),
        P("sec", "bond", None, None),
        P("sec", "bond", None, None, None),
        P("sec", None, None, None),
        P(),
    )
    out_specs = (P("sec", "bond", None, None), P("sec", "bond", None, None, None))
    body = fused if mesh.shape["bond"] == 4 else shards
    return jax.shard_map(body, mesh=mesh, in_specs=in_specs, out_specs=out_specs, check_vma=False)
```

```python
import functools

import jax
import jax.numpy as jnp
from jax import lax
from jax.experimental import pallas as pl
from jax.experimental.pallas import tpu as pltpu
from jax.sharding import PartitionSpec as P

MESH = pl.DeviceIdType.MESH
BF16 = jnp.bfloat16
F32 = jnp.float32


def mm(a, b):
    return jnp.dot(a, b, preferred_element_type=F32)


def kernel(
    dims,
    left_h, site_h, psi_h, right_h, mpo_h,
    new_left, product,
    left, site_raw, psi_raw, mpo, right,
    site_own, psi_own, site, site_tr, mix, pair,
    second, part, rs1, send2, rs2, nl_own, nl_in, psi, mixed, proj, acc,
    local_sem, send_sem, recv_sem,
):
    rows, width, phys, chi, group, cuts, batch = dims
    n_bond = 4
    pq = phys * phys
    sec = lax.axis_index("sec")
    me = lax.axis_index("bond")
    n_sec = lax.axis_size("sec")
    next_sec = lax.rem(sec + 1, n_sec)
    prev_sec = lax.rem(sec + n_sec - 1, n_sec)
    bx = (me // 2) * 2 + 1 - lax.rem(me, 2)
    by = lax.rem(me + 2, n_bond)
    bd = lax.rem(bx + 2, n_bond)
    to_x = {"bond": bx}
    to_y = {"bond": by}
    to_next = {"sec": next_sec}

    def block(owner):
        return pl.ds(pl.multiple_of(owner * rows, rows), rows)

    loads = {}
    for i, (name, src, dst) in enumerate((
        ("site", site_h, site_raw),
        ("psi", psi_h, psi_raw),
        ("mpo", mpo_h, mpo),
        ("left", left_h, left),
        ("right", right_h, right),
    )):
        loads[name] = pltpu.make_async_copy(src, dst, local_sem.at[i])
        loads[name].start()

    barrier = pltpu.get_barrier_semaphore()
    for target in (to_x, to_y, to_next, {"sec": prev_sec}):
        pl.semaphore_signal(barrier, inc=1, device_id=target, device_id_type=MESH)
    pl.semaphore_wait(barrier, 4)

    started = []
    counter = {}

    def slot(key):
        return counter.setdefault(key, len(counter))

    def send(key, src, dst, target):
        i = slot(key)
        copy = pltpu.make_async_remote_copy(
            src_ref=src, dst_ref=dst, send_sem=send_sem.at[i], recv_sem=recv_sem.at[i],
            device_id=target, device_id_type=MESH,
        )
        copy.start()
        started.append(copy)

    def arrive(key, dst, target):
        i = slot(key)
        pltpu.make_async_remote_copy(
            src_ref=dst, dst_ref=dst, send_sem=send_sem.at[i], recv_sem=recv_sem.at[i],
            device_id=target, device_id_type=MESH,
        ).wait_recv()

    lanes = chi // cuts

    loads["site"].wait()
    flat = site_raw[...].astype(F32).reshape(rows * phys, chi)
    for i in range(cuts):
        acc[i, :rows * phys, :] = flat[:, i * lanes:(i + 1) * lanes]
    for t in range(phys):
        for i in range(cuts):
            tile = acc[i, pl.ds(t, rows, stride=phys), :]
            site_own[t, :, i * lanes:(i + 1) * lanes] = tile.astype(BF16)
            site_tr[i * lanes:(i + 1) * lanes, t * rows:(t + 1) * rows] = tile.T.astype(BF16)
    site_here = pltpu.make_async_copy(site_own, site.at[:, block(me), :], local_sem.at[5])
    site_here.start()
    send("site_x", site_own, site.at[:, block(me), :], to_x)
    send("site_y", site_own, site.at[:, block(me), :], to_y)

    loads["psi"].wait()
    tall = 8

    @pl.loop(0, rows // tall)
    def _(g):
        flat = psi_raw[pl.ds(pl.multiple_of(g * tall, tall), tall)].astype(F32)
        flat = flat.reshape(tall * pq, chi)
        where = pl.ds(pl.multiple_of(g * tall * pq, tall * pq), tall * pq)
        for i in range(cuts):
            acc[i, where, :] = flat[:, i * lanes:(i + 1) * lanes]

    half = pq // 4

    def region(q, owner, sub=None):
        if sub is None:
            return psi.at[q, :, block(owner), :]
        return psi.at[q, pl.ds(sub * half, half), block(owner), :]

    for q in range(cuts):
        for t in range(pq):
            at = (t % 2) * lanes
            tile = acc[q, pl.ds(t, rows, stride=pq), :]
            psi_own[q, t // 2, :, at:at + lanes] = tile.astype(BF16)
        if q > 0:
            send(("shift", q - 1), psi_own.at[q - 1], region(q - 1, me), to_next)
    send(("shift", cuts - 1), psi_own.at[cuts - 1], region(cuts - 1, me), to_next)

    def spread(q):
        arrive(("shift", q), region(q, me), to_next)
        send(("psi_x", q), region(q, me), region(q, me), to_x)
        send(("psi_y", q), region(q, me), region(q, me), to_y)

    def relay(q):
        arrive(("psi_x", q), region(q, bx), to_x)
        send(("psi_xy", q), region(q, bx, 0), region(q, bx, 0), to_y)
        arrive(("psi_y", q), region(q, by), to_y)
        send(("psi_yx", q), region(q, by, 1), region(q, by, 1), to_x)

    def complete(q):
        arrive(("psi_xy", q), region(q, bd, 0), to_y)
        arrive(("psi_yx", q), region(q, bd, 1), to_x)

    loads["mpo"].wait()

    def iota(shape, axis):
        return lax.broadcasted_iota(jnp.int32, shape, axis)

    def one_hot(condition):
        return jnp.where(condition, 1.0, 0.0).astype(BF16)

    small = phys * width
    big = small * group
    tall_code = lax.div(iota((big, small), 0), group)
    spread_rows = one_hot(tall_code == iota((big, small), 1))
    col = iota((small, big), 1)
    col_code = lax.div(col, group * width) * width + lax.rem(col, width)
    spread_cols = one_hot(col_code == iota((small, big), 0))
    wide = mm(mm(spread_rows, mpo[...]).astype(BF16), spread_cols)
    same = lax.rem(iota((big, big), 0), group) == lax.rem(lax.div(iota((big, big), 1), width), group)
    mix[...] = jnp.where(same, wide, 0.0).astype(BF16)

    side = width * pq
    col = iota((small, side), 1)
    col_m = lax.rem(col, width)
    col_sv = lax.rem(lax.div(col, width), pq // 2) * 2 + lax.div(col, width * (pq // 2))
    col_s, col_v = lax.div(col_sv, phys), lax.rem(col_sv, phys)
    row = iota((side, small), 0)
    row_k, row_u, row_w = lax.div(row, pq), lax.rem(lax.div(row, phys), phys), lax.rem(row, phys)
    code_c, code_r = iota((small, side), 0), iota((side, small), 1)
    t1 = mm(mpo[...], one_hot(col_s * width + col_m == code_c)).astype(BF16)
    t2 = mm(one_hot(row_w * width + row_k == code_r), mpo[...]).astype(BF16)
    both = jnp.zeros((side, side), F32)
    for n in range(width):
        near = mm(one_hot(row_u * width + n == code_r), t1)
        both += near * mm(t2, one_hot(col_v * width + n == code_c))
    pair[...] = both.astype(BF16)

    cut_s = phys // 2
    lo, hi = pl.ds(0, cut_s), pl.ds(cut_s, phys - cut_s)
    arrive("site_x", site.at[:, block(bx), :], to_x)
    send("site_xy", site.at[lo, block(bx), :], site.at[lo, block(bx), :], to_y)
    arrive("site_y", site.at[:, block(by), :], to_y)
    send("site_yx", site.at[hi, block(by), :], site.at[hi, block(by), :], to_x)
    spread(0)
    loads["left"].wait()
    site_here.wait()
    arrive("site_xy", site.at[lo, block(bd), :], to_y)
    arrive("site_yx", site.at[hi, block(bd), :], to_x)

    strip = group * width

    @pl.loop(0, rows // group)
    def _(g):
        ours = left[pl.ds(pl.multiple_of(g * group, group), group)].astype(F32)
        ours = ours.reshape(strip, chi).astype(BF16)
        first = jnp.concatenate([mm(ours, site[s]).astype(BF16) for s in range(phys)], axis=0)
        out = mm(mix[...], first).astype(BF16)
        for u in range(phys):
            for n in range(width):
                at = (u * width + n) * group
                where = pl.multiple_of(u * rows + g * group, group)
                second[n, pl.ds(where, group), :] = out[at:at + group, :]

    relay(0)
    half_w = width // 2
    order = [k + d * half_w for k in range(half_w) for d in range(2)]

    def first_round(n):
        if n < half_w:
            send(("rs_own", n), part.at[n, block(bx), :], rs1.at[n, 0], to_x)
            send(("rs_far", n), part.at[n, block(bd), :], rs1.at[n, 1], to_x)
        else:
            send(("rs_own", n), part.at[n, block(by), :], rs1.at[n, 0], to_y)
            send(("rs_far", n), part.at[n, block(bd), :], rs1.at[n, 1], to_y)

    behind = None
    for n in order:
        part[n] = mm(site_tr[...], second[n]).astype(BF16)
        if behind is not None:
            first_round(behind)
        behind = n
    first_round(behind)
    spread(1)

    def second_round(n):
        if n < half_w:
            send(("rs_last", n), send2.at[n], rs2.at[n], to_y)
        else:
            send(("rs_last", n), send2.at[n], rs2.at[n], to_x)

    behind = None
    for n in order:
        src, other = (to_x, by) if n < half_w else (to_y, bx)
        arrive(("rs_far", n), rs1.at[n, 1], src)
        send2[n] = (part[n, block(other), :].astype(F32) + rs1[n, 1].astype(F32)).astype(BF16)
        if behind is not None:
            second_round(behind)
        behind = n
    second_round(behind)
    relay(1)
    spread(2)
    for n in order:
        src, last = (to_x, to_y) if n < half_w else (to_y, to_x)
        arrive(("rs_own", n), rs1.at[n, 0], src)
        arrive(("rs_last", n), rs2.at[n], last)
        total = part[n, block(me), :].astype(F32) + rs1[n, 0].astype(F32) + rs2[n].astype(F32)
        for i in range(cuts):
            acc[i, pl.ds(n, rows, stride=width), :] = total[:, i * lanes:(i + 1) * lanes]
    whole = jnp.concatenate([acc[i, :rows * width, :] for i in range(cuts)], axis=1)
    nl_own[...] = whole.astype(BF16)
    new_left[...] = whole.reshape(rows, width, chi).astype(BF16)
    send("left", nl_own, nl_in, to_next)
    relay(2)
    spread(3)
    loads["right"].wait()
    arrive("left", nl_in, to_next)

    for q in range(cuts):
        complete(q)

        def strip_of(g):
            high = batch * width
            ours = nl_in[pl.ds(pl.multiple_of(g * high, high), high), :]

            @pl.loop(0, pq // 2)
            def _(t):
                mixed[t] = mm(ours, psi[q, t])

            @pl.loop(0, batch // 2, unroll=4)
            def _(p):
                here = mixed[:, pl.ds(pl.multiple_of(p * 2 * width, 2 * width), 2 * width), :]
                tiles = []
                for i in range(2):
                    one = here[:, i * width:(i + 1) * width, :].reshape(pq // 2 * width, 2 * lanes)
                    tiles.append(jnp.concatenate([one[:, :lanes], one[:, lanes:]], axis=0))
                both = jnp.concatenate(tiles, axis=1).astype(BF16)
                out = mm(pair[...], both).astype(BF16)
                for i in range(2):
                    where = pl.ds(pl.multiple_of((p * 2 + i) * pq, pq), pq)
                    for k in range(width):
                        piece = out[k * pq:(k + 1) * pq, i * lanes:(i + 1) * lanes]
                        proj[where, k * lanes:(k + 1) * lanes] = piece

            env = right[:, q * lanes:(q + 1) * lanes, :].reshape(width * lanes, chi)
            total = mm(proj[...], env)
            long = pl.ds(pl.multiple_of(g * batch * pq, batch * pq), batch * pq)
            if q > 0:
                total += jnp.concatenate([acc[i, long, :] for i in range(cuts)], axis=1)
            if q < cuts - 1:
                for i in range(cuts):
                    acc[i, long, :] = total[:, i * lanes:(i + 1) * lanes]
            else:
                out = total.reshape(batch, phys, phys, chi).astype(BF16)
                product[pl.ds(pl.multiple_of(g * batch, batch), batch)] = out

        if q == cuts - 2:
            strip_of(0)
            relay(cuts - 1)
            pl.loop(1, rows // batch)(strip_of)
        else:
            pl.loop(0, rows // batch)(strip_of)

    for copy in started:
        copy.wait_send()


def fused(left_env, site, psi, right_env, mpo):
    _, rows, width, chi = left_env.shape
    phys = site.shape[2]
    pq = phys * phys
    group, cuts, batch = 16, 4, 64
    lanes = chi // cuts
    small = phys * width
    table = mpo.transpose(3, 1, 2, 0).reshape(small, small)
    n_sems = 80
    any_spec = pl.BlockSpec(memory_space=pl.ANY)
    vmem = pl.BlockSpec(memory_space=pltpu.VMEM)
    new_left, product = pl.pallas_call(
        functools.partial(kernel, (rows, width, phys, chi, group, cuts, batch)),
        out_shape=(
            jax.ShapeDtypeStruct((rows, width, chi), BF16),
            jax.ShapeDtypeStruct((rows, phys, phys, chi), BF16),
        ),
        in_specs=[any_spec] * 5,
        out_specs=(vmem, vmem),
        scratch_shapes=[
            pltpu.VMEM((rows, width, chi), BF16),
            pltpu.VMEM((rows, phys, chi), BF16),
            pltpu.VMEM((rows, phys, phys, chi), BF16),
            pltpu.VMEM((small, small), BF16),
            pltpu.VMEM((width, chi, chi), BF16),
            pltpu.VMEM((phys, rows, chi), BF16),
            pltpu.VMEM((cuts, pq // 2, rows, 2 * lanes), BF16),
            pltpu.VMEM((phys, chi, chi), BF16),
            pltpu.VMEM((chi, phys * rows), BF16),
            pltpu.VMEM((small * group, small * group), BF16),
            pltpu.VMEM((width * pq, width * pq), BF16),
            pltpu.VMEM((width, phys * rows, chi), BF16),
            pltpu.VMEM((width, chi, chi), BF16),
            pltpu.VMEM((width, 2, rows, chi), BF16),
            pltpu.VMEM((width, rows, chi), BF16),
            pltpu.VMEM((width, rows, chi), BF16),
            pltpu.VMEM((rows * width, chi), BF16),
            pltpu.VMEM((rows * width, chi), BF16),
            pltpu.VMEM((cuts, pq // 2, chi, 2 * lanes), BF16),
            pltpu.VMEM((pq // 2, batch * width, 2 * lanes), F32),
            pltpu.VMEM((batch * pq, width * lanes), BF16),
            pltpu.VMEM((cuts, rows * pq, lanes), F32),
            pltpu.SemaphoreType.DMA((6,)),
            pltpu.SemaphoreType.DMA((n_sems,)),
            pltpu.SemaphoreType.DMA((n_sems,)),
        ],
        compiler_params=pltpu.CompilerParams(
            collective_id=0, has_side_effects=True, vmem_limit_bytes=62 * 1024 * 1024
        ),
    )(left_env[0], site[0], psi[0], right_env[0], table)
    return new_left[None], product[None]


def shifted(block, axis, distance):
    devices = range(lax.axis_size(axis))
    route = [((i - distance) % len(devices), i) for i in devices]
    return lax.ppermute(block, axis, route)


def shards(left_env, site, psi, right_env, mpo):
    left = left_env[0]
    tensor = site[0]
    rows = tensor.shape[0]
    phys = tensor.shape[1]
    chi = tensor.shape[2]
    width = left.shape[1]
    pair_source = shifted(psi[0], "sec", 1)
    offset = lax.axis_index("bond") * rows
    whole_left, whole_site = (
        lax.all_gather(left, "bond", axis=0, tiled=True),
        lax.all_gather(tensor, "bond", axis=0, tiled=True),
    )
    own_cols = lax.dynamic_slice_in_dim(whole_site, offset, rows, 2)
    first = jnp.dot(
        whole_left.reshape(chi * width, chi),
        own_cols.reshape(chi, phys * rows),
        preferred_element_type=jnp.float32,
    )
    first = first.astype(jnp.bfloat16).reshape(chi, width, phys, rows)
    second = jnp.einsum("pmsb,mnsu->punb", first, mpo, preferred_element_type=jnp.float32).astype(
        jnp.bfloat16
    )
    fresh = lax.dot_general(
        whole_site.reshape(chi * phys, chi),
        second.reshape(chi * phys, width * rows),
        (((0,), (0,)), ((), ())),
        preferred_element_type=jnp.float32,
    )
    fresh = fresh.astype(jnp.bfloat16).reshape(chi, width, rows)
    new_left = lax.all_to_all(fresh, "bond", split_axis=0, concat_axis=2, tiled=True)
    left_source = shifted(new_left, "sec", 1)
    source_flat = left_source.reshape(rows * width, chi)
    pair = pair_source.reshape(rows, phys * phys * chi)
    mixed = jnp.dot(
        source_flat,
        lax.all_gather(pair, "bond", axis=0, tiled=True),
        preferred_element_type=jnp.float32,
    )
    mixed = mixed.astype(jnp.bfloat16).reshape(rows, width * phys * phys, chi)
    two_site = jnp.einsum("mnsu,nkvw->msvuwk", mpo, mpo, preferred_element_type=jnp.float32)
    two_site = two_site.astype(jnp.bfloat16).reshape(width * phys * phys, phys * phys * width)
    projected = jnp.einsum(
        "pqc,qr->prc", mixed, two_site, preferred_element_type=jnp.float32
    ).astype(jnp.bfloat16)
    env_right = right_env[0].reshape(width * chi, chi)
    result = jnp.dot(
        projected.reshape(rows * phys * phys, width * chi),
        env_right,
        preferred_element_type=jnp.float32,
    ).astype(jnp.bfloat16)
    return (new_left[None], result.reshape(1, rows, phys, phys, chi))


def solution(mesh):
    in_specs = (
        P("sec", "bond", None, None),
        P("sec", "bond", None, None),
        P("sec", "bond", None, None, None),
        P("sec", None, None, None),
        P(),
    )
    out_specs = (P("sec", "bond", None, None), P("sec", "bond", None, None, None))
    body = fused if mesh.shape["bond"] == 4 else shards
    return jax.shard_map(body, mesh=mesh, in_specs=in_specs, out_specs=out_specs, check_vma=False)
```

```python
import functools

import jax
import jax.numpy as jnp
from jax import lax
from jax.experimental import pallas as pl
from jax.experimental.pallas import tpu as pltpu
from jax.sharding import PartitionSpec as P

MESH = pl.DeviceIdType.MESH
BF16 = jnp.bfloat16
F32 = jnp.float32


def mm(a, b):
    return jnp.dot(a, b, preferred_element_type=F32)


def kernel(
    dims,
    left_h, site_h, psi_h, right_h, mpo_h,
    new_left, product,
    left, site_raw, psi_raw, mpo, right,
    site_own, psi_own, site, site_tr, mix, pair,
    second, part, rs1, send2, rs2, nl_own, nl_in, psi, mixed, proj, acc,
    local_sem, send_sem, recv_sem,
):
    rows, width, phys, chi, group, cuts, batch = dims
    n_bond = 4
    pq = phys * phys
    sec = lax.axis_index("sec")
    me = lax.axis_index("bond")
    n_sec = lax.axis_size("sec")
    next_sec = lax.rem(sec + 1, n_sec)
    prev_sec = lax.rem(sec + n_sec - 1, n_sec)
    bx = (me // 2) * 2 + 1 - lax.rem(me, 2)
    by = lax.rem(me + 2, n_bond)
    bd = lax.rem(bx + 2, n_bond)
    to_x = {"bond": bx}
    to_y = {"bond": by}
    to_next = {"sec": next_sec}

    def block(owner):
        return pl.ds(pl.multiple_of(owner * rows, rows), rows)

    loads = {}
    for i, (name, src, dst) in enumerate((
        ("site", site_h, site_raw),
        ("psi", psi_h, psi_raw),
        ("mpo", mpo_h, mpo),
        ("left", left_h, left),
        ("right", right_h, right),
    )):
        loads[name] = pltpu.make_async_copy(src, dst, local_sem.at[i])
        loads[name].start()

    barrier = pltpu.get_barrier_semaphore()
    for target in (to_x, to_y, to_next, {"sec": prev_sec}):
        pl.semaphore_signal(barrier, inc=1, device_id=target, device_id_type=MESH)
    pl.semaphore_wait(barrier, 4)

    started = []
    counter = {}

    def slot(key):
        return counter.setdefault(key, len(counter))

    def send(key, src, dst, target):
        i = slot(key)
        copy = pltpu.make_async_remote_copy(
            src_ref=src, dst_ref=dst, send_sem=send_sem.at[i], recv_sem=recv_sem.at[i],
            device_id=target, device_id_type=MESH,
        )
        copy.start()
        started.append(copy)

    def arrive(key, dst, target):
        i = slot(key)
        pltpu.make_async_remote_copy(
            src_ref=dst, dst_ref=dst, send_sem=send_sem.at[i], recv_sem=recv_sem.at[i],
            device_id=target, device_id_type=MESH,
        ).wait_recv()

    lanes = chi // cuts

    loads["site"].wait()
    flat = site_raw[...].astype(F32).reshape(rows * phys, chi)
    for i in range(cuts):
        acc[i, :rows * phys, :] = flat[:, i * lanes:(i + 1) * lanes]
    for t in range(phys):
        for i in range(cuts):
            tile = acc[i, pl.ds(t, rows, stride=phys), :]
            site_own[t, :, i * lanes:(i + 1) * lanes] = tile.astype(BF16)
            site_tr[i * lanes:(i + 1) * lanes, t * rows:(t + 1) * rows] = tile.T.astype(BF16)
    site_here = pltpu.make_async_copy(site_own, site.at[:, block(me), :], local_sem.at[5])
    site_here.start()
    send("site_x", site_own, site.at[:, block(me), :], to_x)
    send("site_y", site_own, site.at[:, block(me), :], to_y)

    loads["psi"].wait()
    tall = 8

    @pl.loop(0, rows // tall)
    def _(g):
        flat = psi_raw[pl.ds(pl.multiple_of(g * tall, tall), tall)].astype(F32)
        flat = flat.reshape(tall * pq, chi)
        where = pl.ds(pl.multiple_of(g * tall * pq, tall * pq), tall * pq)
        for i in range(cuts):
            acc[i, where, :] = flat[:, i * lanes:(i + 1) * lanes]

    half = pq // 4

    def region(q, owner, sub=None):
        if sub is None:
            return psi.at[q, :, block(owner), :]
        return psi.at[q, pl.ds(sub * half, half), block(owner), :]

    for q in range(cuts):
        for t in range(pq):
            at = (t % 2) * lanes
            tile = acc[q, pl.ds(t, rows, stride=pq), :]
            psi_own[q, t // 2, :, at:at + lanes] = tile.astype(BF16)
        if q > 0:
            send(("shift", q - 1), psi_own.at[q - 1], region(q - 1, me), to_next)
    send(("shift", cuts - 1), psi_own.at[cuts - 1], region(cuts - 1, me), to_next)

    def spread(q):
        arrive(("shift", q), region(q, me), to_next)
        send(("psi_x", q), region(q, me), region(q, me), to_x)
        send(("psi_y", q), region(q, me), region(q, me), to_y)

    def relay(q):
        arrive(("psi_x", q), region(q, bx), to_x)
        send(("psi_xy", q), region(q, bx, 0), region(q, bx, 0), to_y)
        arrive(("psi_y", q), region(q, by), to_y)
        send(("psi_yx", q), region(q, by, 1), region(q, by, 1), to_x)

    def complete(q):
        arrive(("psi_xy", q), region(q, bd, 0), to_y)
        arrive(("psi_yx", q), region(q, bd, 1), to_x)

    loads["mpo"].wait()

    def iota(shape, axis):
        return lax.broadcasted_iota(jnp.int32, shape, axis)

    def one_hot(condition):
        return jnp.where(condition, 1.0, 0.0).astype(BF16)

    small = phys * width
    big = small * group
    tall_code = lax.div(iota((big, small), 0), group)
    spread_rows = one_hot(tall_code == iota((big, small), 1))
    col = iota((small, big), 1)
    col_code = lax.div(col, group * width) * width + lax.rem(col, width)
    spread_cols = one_hot(col_code == iota((small, big), 0))
    wide = mm(mm(spread_rows, mpo[...]).astype(BF16), spread_cols)
    same = lax.rem(iota((big, big), 0), group) == lax.rem(lax.div(iota((big, big), 1), width), group)
    mix[...] = jnp.where(same, wide, 0.0).astype(BF16)

    side = width * pq
    col = iota((small, side), 1)
    col_m = lax.rem(col, width)
    col_sv = lax.rem(lax.div(col, width), pq // 2) * 2 + lax.div(col, width * (pq // 2))
    col_s, col_v = lax.div(col_sv, phys), lax.rem(col_sv, phys)
    row = iota((side, small), 0)
    row_k, row_u, row_w = lax.div(row, pq), lax.rem(lax.div(row, phys), phys), lax.rem(row, phys)
    code_c, code_r = iota((small, side), 0), iota((side, small), 1)
    t1 = mm(mpo[...], one_hot(col_s * width + col_m == code_c)).astype(BF16)
    t2 = mm(one_hot(row_w * width + row_k == code_r), mpo[...]).astype(BF16)
    both = jnp.zeros((side, side), F32)
    for n in range(width):
        near = mm(one_hot(row_u * width + n == code_r), t1)
        both += near * mm(t2, one_hot(col_v * width + n == code_c))
    pair[...] = both.astype(BF16)

    cut_s = phys // 2
    lo, hi = pl.ds(0, cut_s), pl.ds(cut_s, phys - cut_s)
    arrive("site_x", site.at[:, block(bx), :], to_x)
    send("site_xy", site.at[lo, block(bx), :], site.at[lo, block(bx), :], to_y)
    arrive("site_y", site.at[:, block(by), :], to_y)
    send("site_yx", site.at[hi, block(by), :], site.at[hi, block(by), :], to_x)
    spread(0)
    loads["left"].wait()
    site_here.wait()
    arrive("site_xy", site.at[lo, block(bd), :], to_y)
    arrive("site_yx", site.at[hi, block(bd), :], to_x)

    strip = group * width

    @pl.loop(0, rows // group)
    def _(g):
        ours = left[pl.ds(pl.multiple_of(g * group, group), group)].astype(F32)
        ours = ours.reshape(strip, chi).astype(BF16)
        first = jnp.concatenate([mm(ours, site[s]).astype(BF16) for s in range(phys)], axis=0)
        out = mm(mix[...], first).astype(BF16)
        for u in range(phys):
            for n in range(width):
                at = (u * width + n) * group
                where = pl.multiple_of(u * rows + g * group, group)
                second[n, pl.ds(where, group), :] = out[at:at + group, :]

    half_w = width // 2
    order = [k + d * half_w for k in range(half_w) for d in range(2)]

    def first_round(n):
        if n < half_w:
            send(("rs_own", n), part.at[n, block(bx), :], rs1.at[n, 0], to_x)
            send(("rs_far", n), part.at[n, block(bd), :], rs1.at[n, 1], to_x)
        else:
            send(("rs_own", n), part.at[n, block(by), :], rs1.at[n, 0], to_y)
            send(("rs_far", n), part.at[n, block(bd), :], rs1.at[n, 1], to_y)

    behind = None
    for n in order:
        part[n] = mm(site_tr[...], second[n]).astype(BF16)
        if behind is not None:
            first_round(behind)
        behind = n
    first_round(behind)

    def second_round(n):
        if n < half_w:
            send(("rs_last", n), send2.at[n], rs2.at[n], to_y)
        else:
            send(("rs_last", n), send2.at[n], rs2.at[n], to_x)

    behind = None
    for n in order:
        src, other = (to_x, by) if n < half_w else (to_y, bx)
        arrive(("rs_far", n), rs1.at[n, 1], src)
        send2[n] = (part[n, block(other), :].astype(F32) + rs1[n, 1].astype(F32)).astype(BF16)
        if behind is not None:
            second_round(behind)
        behind = n
    second_round(behind)
    relay(0)
    spread(1)
    for n in order:
        src, last = (to_x, to_y) if n < half_w else (to_y, to_x)
        arrive(("rs_own", n), rs1.at[n, 0], src)
        arrive(("rs_last", n), rs2.at[n], last)
        total = part[n, block(me), :].astype(F32) + rs1[n, 0].astype(F32) + rs2[n].astype(F32)
        for i in range(cuts):
            acc[i, pl.ds(n, rows, stride=width), :] = total[:, i * lanes:(i + 1) * lanes]
    whole = jnp.concatenate([acc[i, :rows * width, :] for i in range(cuts)], axis=1)
    nl_own[...] = whole.astype(BF16)
    new_left[...] = whole.reshape(rows, width, chi).astype(BF16)
    send("left", nl_own, nl_in, to_next)
    relay(1)
    spread(2)
    loads["right"].wait()
    arrive("left", nl_in, to_next)

    for q in range(cuts):
        complete(q)

        def strip_of(g):
            high = batch * width
            ours = nl_in[pl.ds(pl.multiple_of(g * high, high), high), :]

            @pl.loop(0, pq // 2)
            def _(t):
                mixed[t] = mm(ours, psi[q, t])

            @pl.loop(0, batch // 2, unroll=4)
            def _(p):
                here = mixed[:, pl.ds(pl.multiple_of(p * 2 * width, 2 * width), 2 * width), :]
                tiles = []
                for i in range(2):
                    one = here[:, i * width:(i + 1) * width, :].reshape(pq // 2 * width, 2 * lanes)
                    tiles.append(jnp.concatenate([one[:, :lanes], one[:, lanes:]], axis=0))
                both = jnp.concatenate(tiles, axis=1).astype(BF16)
                out = mm(pair[...], both).astype(BF16)
                for i in range(2):
                    where = pl.ds(pl.multiple_of((p * 2 + i) * pq, pq), pq)
                    for k in range(width):
                        piece = out[k * pq:(k + 1) * pq, i * lanes:(i + 1) * lanes]
                        proj[where, k * lanes:(k + 1) * lanes] = piece

            env = right[:, q * lanes:(q + 1) * lanes, :].reshape(width * lanes, chi)
            total = mm(proj[...], env)
            long = pl.ds(pl.multiple_of(g * batch * pq, batch * pq), batch * pq)
            if q > 0:
                total += jnp.concatenate([acc[i, long, :] for i in range(cuts)], axis=1)
            if q < cuts - 1:
                for i in range(cuts):
                    acc[i, long, :] = total[:, i * lanes:(i + 1) * lanes]
            else:
                out = total.reshape(batch, phys, phys, chi).astype(BF16)
                product[pl.ds(pl.multiple_of(g * batch, batch), batch)] = out

        if 0 < q < cuts - 1:
            strip_of(0)
            relay(q + 1)
            if q + 2 < cuts:
                spread(q + 2)
            pl.loop(1, rows // batch)(strip_of)
        else:
            pl.loop(0, rows // batch)(strip_of)

    for copy in started:
        copy.wait_send()


def fused(left_env, site, psi, right_env, mpo):
    _, rows, width, chi = left_env.shape
    phys = site.shape[2]
    pq = phys * phys
    group, cuts, batch = 16, 4, 64
    lanes = chi // cuts
    small = phys * width
    table = mpo.transpose(3, 1, 2, 0).reshape(small, small)
    n_sems = 80
    any_spec = pl.BlockSpec(memory_space=pl.ANY)
    vmem = pl.BlockSpec(memory_space=pltpu.VMEM)
    new_left, product = pl.pallas_call(
        functools.partial(kernel, (rows, width, phys, chi, group, cuts, batch)),
        out_shape=(
            jax.ShapeDtypeStruct((rows, width, chi), BF16),
            jax.ShapeDtypeStruct((rows, phys, phys, chi), BF16),
        ),
        in_specs=[any_spec] * 5,
        out_specs=(vmem, vmem),
        scratch_shapes=[
            pltpu.VMEM((rows, width, chi), BF16),
            pltpu.VMEM((rows, phys, chi), BF16),
            pltpu.VMEM((rows, phys, phys, chi), BF16),
            pltpu.VMEM((small, small), BF16),
            pltpu.VMEM((width, chi, chi), BF16),
            pltpu.VMEM((phys, rows, chi), BF16),
            pltpu.VMEM((cuts, pq // 2, rows, 2 * lanes), BF16),
            pltpu.VMEM((phys, chi, chi), BF16),
            pltpu.VMEM((chi, phys * rows), BF16),
            pltpu.VMEM((small * group, small * group), BF16),
            pltpu.VMEM((width * pq, width * pq), BF16),
            pltpu.VMEM((width, phys * rows, chi), BF16),
            pltpu.VMEM((width, chi, chi), BF16),
            pltpu.VMEM((width, 2, rows, chi), BF16),
            pltpu.VMEM((width, rows, chi), BF16),
            pltpu.VMEM((width, rows, chi), BF16),
            pltpu.VMEM((rows * width, chi), BF16),
            pltpu.VMEM((rows * width, chi), BF16),
            pltpu.VMEM((cuts, pq // 2, chi, 2 * lanes), BF16),
            pltpu.VMEM((pq // 2, batch * width, 2 * lanes), F32),
            pltpu.VMEM((batch * pq, width * lanes), BF16),
            pltpu.VMEM((cuts, rows * pq, lanes), F32),
            pltpu.SemaphoreType.DMA((6,)),
            pltpu.SemaphoreType.DMA((n_sems,)),
            pltpu.SemaphoreType.DMA((n_sems,)),
        ],
        compiler_params=pltpu.CompilerParams(
            collective_id=0, has_side_effects=True, vmem_limit_bytes=62 * 1024 * 1024
        ),
    )(left_env[0], site[0], psi[0], right_env[0], table)
    return new_left[None], product[None]


def shifted(block, axis, distance):
    devices = range(lax.axis_size(axis))
    route = [((i - distance) % len(devices), i) for i in devices]
    return lax.ppermute(block, axis, route)


def shards(left_env, site, psi, right_env, mpo):
    left = left_env[0]
    tensor = site[0]
    rows = tensor.shape[0]
    phys = tensor.shape[1]
    chi = tensor.shape[2]
    width = left.shape[1]
    pair_source = shifted(psi[0], "sec", 1)
    offset = lax.axis_index("bond") * rows
    whole_left, whole_site = (
        lax.all_gather(left, "bond", axis=0, tiled=True),
        lax.all_gather(tensor, "bond", axis=0, tiled=True),
    )
    own_cols = lax.dynamic_slice_in_dim(whole_site, offset, rows, 2)
    first = jnp.dot(
        whole_left.reshape(chi * width, chi),
        own_cols.reshape(chi, phys * rows),
        preferred_element_type=jnp.float32,
    )
    first = first.astype(jnp.bfloat16).reshape(chi, width, phys, rows)
    second = jnp.einsum("pmsb,mnsu->punb", first, mpo, preferred_element_type=jnp.float32).astype(
        jnp.bfloat16
    )
    fresh = lax.dot_general(
        whole_site.reshape(chi * phys, chi),
        second.reshape(chi * phys, width * rows),
        (((0,), (0,)), ((), ())),
        preferred_element_type=jnp.float32,
    )
    fresh = fresh.astype(jnp.bfloat16).reshape(chi, width, rows)
    new_left = lax.all_to_all(fresh, "bond", split_axis=0, concat_axis=2, tiled=True)
    left_source = shifted(new_left, "sec", 1)
    source_flat = left_source.reshape(rows * width, chi)
    pair = pair_source.reshape(rows, phys * phys * chi)
    mixed = jnp.dot(
        source_flat,
        lax.all_gather(pair, "bond", axis=0, tiled=True),
        preferred_element_type=jnp.float32,
    )
    mixed = mixed.astype(jnp.bfloat16).reshape(rows, width * phys * phys, chi)
    two_site = jnp.einsum("mnsu,nkvw->msvuwk", mpo, mpo, preferred_element_type=jnp.float32)
    two_site = two_site.astype(jnp.bfloat16).reshape(width * phys * phys, phys * phys * width)
    projected = jnp.einsum(
        "pqc,qr->prc", mixed, two_site, preferred_element_type=jnp.float32
    ).astype(jnp.bfloat16)
    env_right = right_env[0].reshape(width * chi, chi)
    result = jnp.dot(
        projected.reshape(rows * phys * phys, width * chi),
        env_right,
        preferred_element_type=jnp.float32,
    ).astype(jnp.bfloat16)
    return (new_left[None], result.reshape(1, rows, phys, phys, chi))


def solution(mesh):
    in_specs = (
        P("sec", "bond", None, None),
        P("sec", "bond", None, None),
        P("sec", "bond", None, None, None),
        P("sec", None, None, None),
        P(),
    )
    out_specs = (P("sec", "bond", None, None), P("sec", "bond", None, None, None))
    body = fused if mesh.shape["bond"] == 4 else shards
    return jax.shard_map(body, mesh=mesh, in_specs=in_specs, out_specs=out_specs, check_vma=False)
```

```python
import functools

import jax
import jax.numpy as jnp
from jax import lax
from jax.experimental import pallas as pl
from jax.experimental.pallas import tpu as pltpu
from jax.sharding import PartitionSpec as P

MESH = pl.DeviceIdType.MESH
BF16 = jnp.bfloat16
F32 = jnp.float32


def mm(a, b):
    return jnp.dot(a, b, preferred_element_type=F32)


def kernel(
    dims,
    left_h, site_h, psi_h, right_h, mpo_h,
    new_left, product,
    left, site_raw, psi_raw, mpo, right,
    site_own, psi_own, site, site_tr, mix, pair,
    second, part, rs1, send2, rs2, nl_own, nl_in, psi, mixed, proj, acc,
    local_sem, send_sem, recv_sem,
):
    rows, width, phys, chi, group, cuts, batch = dims
    n_bond = 4
    pq = phys * phys
    sec = lax.axis_index("sec")
    me = lax.axis_index("bond")
    n_sec = lax.axis_size("sec")
    next_sec = lax.rem(sec + 1, n_sec)
    prev_sec = lax.rem(sec + n_sec - 1, n_sec)
    bx = (me // 2) * 2 + 1 - lax.rem(me, 2)
    by = lax.rem(me + 2, n_bond)
    bd = lax.rem(bx + 2, n_bond)
    x, y = lax.rem(me, 2), me // 2
    to_x = {"bond": bx}
    to_y = {"bond": by}
    to_next = {"sec": next_sec}

    def block(owner):
        return pl.ds(pl.multiple_of(owner * rows, rows), rows)

    loads = {}
    for i, (name, src, dst) in enumerate((
        ("site", site_h, site_raw),
        ("psi", psi_h, psi_raw),
        ("mpo", mpo_h, mpo),
        ("left", left_h, left.at[x]),
        ("right", right_h, right),
    )):
        loads[name] = pltpu.make_async_copy(src, dst, local_sem.at[i])
        loads[name].start()

    barrier = pltpu.get_barrier_semaphore()
    for target in (to_x, to_y, to_next, {"sec": prev_sec}):
        pl.semaphore_signal(barrier, inc=1, device_id=target, device_id_type=MESH)
    pl.semaphore_wait(barrier, 4)

    started = []
    counter = {}

    def slot(key):
        return counter.setdefault(key, len(counter))

    def send(key, src, dst, target):
        i = slot(key)
        copy = pltpu.make_async_remote_copy(
            src_ref=src, dst_ref=dst, send_sem=send_sem.at[i], recv_sem=recv_sem.at[i],
            device_id=target, device_id_type=MESH,
        )
        copy.start()
        started.append(copy)

    def arrive(key, dst, target):
        i = slot(key)
        pltpu.make_async_remote_copy(
            src_ref=dst, dst_ref=dst, send_sem=send_sem.at[i], recv_sem=recv_sem.at[i],
            device_id=target, device_id_type=MESH,
        ).wait_recv()

    lanes = chi // cuts

    loads["site"].wait()
    flat = site_raw[...].astype(F32).reshape(rows * phys, chi)
    for i in range(cuts):
        acc[i, :rows * phys, :] = flat[:, i * lanes:(i + 1) * lanes]
    for t in range(phys):
        for i in range(cuts):
            tile = acc[i, pl.ds(t, rows, stride=phys), :]
            site_own[t, :, i * lanes:(i + 1) * lanes] = tile.astype(BF16)
            site_tr[x, i * lanes:(i + 1) * lanes, t * rows:(t + 1) * rows] = tile.T.astype(BF16)
    site_here = pltpu.make_async_copy(site_own, site.at[:, block(me), :], local_sem.at[5])
    site_here.start()
    send("site_x", site_own, site.at[:, block(me), :], to_x)
    send("left_x", left_h, left.at[x], to_x)

    loads["psi"].wait()
    tall = 8

    @pl.loop(0, rows // tall)
    def _(g):
        flat = psi_raw[pl.ds(pl.multiple_of(g * tall, tall), tall)].astype(F32)
        flat = flat.reshape(tall * pq, chi)
        where = pl.ds(pl.multiple_of(g * tall * pq, tall * pq), tall * pq)
        for i in range(cuts):
            acc[i, where, :] = flat[:, i * lanes:(i + 1) * lanes]

    half = pq // 4

    def region(q, owner, sub=None):
        if sub is None:
            return psi.at[q, :, block(owner), :]
        return psi.at[q, pl.ds(sub * half, half), block(owner), :]

    for q in range(cuts):
        for t in range(pq):
            at = (t % 2) * lanes
            tile = acc[q, pl.ds(t, rows, stride=pq), :]
            psi_own[q, t // 2, :, at:at + lanes] = tile.astype(BF16)
        if q > 0:
            send(("shift", q - 1), psi_own.at[q - 1], region(q - 1, me), to_next)
    send(("shift", cuts - 1), psi_own.at[cuts - 1], region(cuts - 1, me), to_next)

    def spread(q):
        arrive(("shift", q), region(q, me), to_next)
        send(("psi_x", q), region(q, me), region(q, me), to_x)
        send(("psi_y", q), region(q, me), region(q, me), to_y)

    def relay(q):
        arrive(("psi_x", q), region(q, bx), to_x)
        send(("psi_xy", q), region(q, bx, 0), region(q, bx, 0), to_y)
        arrive(("psi_y", q), region(q, by), to_y)
        send(("psi_yx", q), region(q, by, 1), region(q, by, 1), to_x)

    def complete(q):
        arrive(("psi_xy", q), region(q, bd, 0), to_y)
        arrive(("psi_yx", q), region(q, bd, 1), to_x)

    loads["mpo"].wait()

    def iota(shape, axis):
        return lax.broadcasted_iota(jnp.int32, shape, axis)

    def one_hot(condition):
        return jnp.where(condition, 1.0, 0.0).astype(BF16)

    small = phys * width
    big = small * group
    tall_code = lax.div(iota((big, small), 0), group)
    spread_rows = one_hot(tall_code == iota((big, small), 1))
    col = iota((small, big), 1)
    col_code = lax.div(col, group * width) * width + lax.rem(col, width)
    spread_cols = one_hot(col_code == iota((small, big), 0))
    wide = mm(mm(spread_rows, mpo[...]).astype(BF16), spread_cols)
    same = lax.rem(iota((big, big), 0), group) == lax.rem(lax.div(iota((big, big), 1), width), group)
    mix[...] = jnp.where(same, wide, 0.0).astype(BF16)

    side = width * pq
    col = iota((small, side), 1)
    col_m = lax.rem(col, width)
    col_sv = lax.rem(lax.div(col, width), pq // 2) * 2 + lax.div(col, width * (pq // 2))
    col_s, col_v = lax.div(col_sv, phys), lax.rem(col_sv, phys)
    row = iota((side, small), 0)
    row_k, row_u, row_w = lax.div(row, pq), lax.rem(lax.div(row, phys), phys), lax.rem(row, phys)
    code_c, code_r = iota((small, side), 0), iota((side, small), 1)
    t1 = mm(mpo[...], one_hot(col_s * width + col_m == code_c)).astype(BF16)
    t2 = mm(one_hot(row_w * width + row_k == code_r), mpo[...]).astype(BF16)
    both = jnp.zeros((side, side), F32)
    for n in range(width):
        near = mm(one_hot(row_u * width + n == code_r), t1)
        both += near * mm(t2, one_hot(col_v * width + n == code_c))
    pair[...] = both.astype(BF16)

    wide_b = chi // 2
    cols = pl.ds(pl.multiple_of(x * wide_b, wide_b), wide_b)

    def pair_rows(which):
        return pl.ds(pl.multiple_of(which * 2 * rows, 2 * rows), 2 * rows)

    site_here.wait()
    arrive("site_x", site.at[:, block(bx), :], to_x)
    ours = site.at[:, pair_rows(y), cols]
    send("site_pair", ours, ours, to_y)
    for t in range(phys):
        for i in range(cuts):
            tile = site[t, block(bx), i * lanes:(i + 1) * lanes].astype(F32)
            place = (slice(i * lanes, (i + 1) * lanes), slice(t * rows, (t + 1) * rows))
            site_tr[(1 - x,) + place] = tile.T.astype(BF16)
    spread(0)
    loads["left"].wait()
    arrive("site_pair", site.at[:, pair_rows(1 - y), cols], to_y)

    strip = group * width

    def fill(which):
        @pl.loop(0, rows // group)
        def _(g):
            ours = left[which, pl.ds(pl.multiple_of(g * group, group), group)].astype(F32)
            ours = ours.reshape(strip, chi).astype(BF16)
            first = [mm(ours, site[t, :, cols]).astype(BF16) for t in range(phys)]
            out = mm(mix[...], jnp.concatenate(first, axis=0)).astype(BF16)
            for u in range(phys):
                for n in range(width):
                    at = (u * width + n) * group
                    where = pl.multiple_of(u * rows + g * group, group)
                    second[n, which, pl.ds(where, group), :] = out[at:at + group, :]

    fill(x)
    arrive("left_x", left.at[1 - x], to_x)
    fill(1 - x)

    def first_round(n):
        send(("rs", n), part.at[n, pair_rows(1 - y), :], rs1.at[n], to_y)

    def second_round(n):
        send(("swap", n), send2.at[n], rs2.at[n], to_x)

    for n in range(width):
        part[n] = (mm(site_tr[0], second[n, 0]) + mm(site_tr[1], second[n, 1])).astype(BF16)
        if n > 0:
            first_round(n - 1)
    first_round(width - 1)

    def block_in_pair(which):
        return pl.ds(pl.multiple_of(which * rows, rows), rows)

    for n in range(width):
        arrive(("rs", n), rs1.at[n], to_y)
        far = part[n, block(bx), :].astype(F32) + rs1[n, block_in_pair(1 - x), :].astype(F32)
        send2[n] = far.astype(BF16)
        own = part[n, block(me), :].astype(F32) + rs1[n, block_in_pair(x), :].astype(F32)
        for i in range(cuts // 2):
            acc[x * (cuts // 2) + i, pl.ds(n, rows, stride=width), :] = own[:, i * lanes:(i + 1) * lanes]
        if n > 0:
            second_round(n - 1)
    second_round(width - 1)
    relay(0)
    spread(1)
    for n in range(width):
        arrive(("swap", n), rs2.at[n], to_x)
        other = rs2[n].astype(F32)
        for i in range(cuts // 2):
            at = (1 - x) * (cuts // 2) + i
            acc[at, pl.ds(n, rows, stride=width), :] = other[:, i * lanes:(i + 1) * lanes]
    whole = jnp.concatenate([acc[i, :rows * width, :] for i in range(cuts)], axis=1)
    nl_own[...] = whole.astype(BF16)
    new_left[...] = whole.reshape(rows, width, chi).astype(BF16)
    send("left", nl_own, nl_in, to_next)
    relay(1)
    spread(2)
    loads["right"].wait()
    arrive("left", nl_in, to_next)

    for q in range(cuts):
        complete(q)

        def strip_of(g):
            high = batch * width
            ours = nl_in[pl.ds(pl.multiple_of(g * high, high), high), :]

            @pl.loop(0, pq // 2)
            def _(t):
                mixed[t] = mm(ours, psi[q, t])

            @pl.loop(0, batch // 2, unroll=4)
            def _(p):
                here = mixed[:, pl.ds(pl.multiple_of(p * 2 * width, 2 * width), 2 * width), :]
                tiles = []
                for i in range(2):
                    one = here[:, i * width:(i + 1) * width, :].reshape(pq // 2 * width, 2 * lanes)
                    tiles.append(jnp.concatenate([one[:, :lanes], one[:, lanes:]], axis=0))
                both = jnp.concatenate(tiles, axis=1).astype(BF16)
                out = mm(pair[...], both).astype(BF16)
                for i in range(2):
                    where = pl.ds(pl.multiple_of((p * 2 + i) * pq, pq), pq)
                    for k in range(width):
                        piece = out[k * pq:(k + 1) * pq, i * lanes:(i + 1) * lanes]
                        proj[where, k * lanes:(k + 1) * lanes] = piece

            env = right[:, q * lanes:(q + 1) * lanes, :].reshape(width * lanes, chi)
            total = mm(proj[...], env)
            long = pl.ds(pl.multiple_of(g * batch * pq, batch * pq), batch * pq)
            if q > 0:
                total += jnp.concatenate([acc[i, long, :] for i in range(cuts)], axis=1)
            if q < cuts - 1:
                for i in range(cuts):
                    acc[i, long, :] = total[:, i * lanes:(i + 1) * lanes]
            else:
                out = total.reshape(batch, phys, phys, chi).astype(BF16)
                product[pl.ds(pl.multiple_of(g * batch, batch), batch)] = out

        if 0 < q < cuts - 1:
            strip_of(0)
            relay(q + 1)
            if q + 2 < cuts:
                spread(q + 2)
            pl.loop(1, rows // batch)(strip_of)
        else:
            pl.loop(0, rows // batch)(strip_of)

    for copy in started:
        copy.wait_send()


def fused(left_env, site, psi, right_env, mpo):
    _, rows, width, chi = left_env.shape
    phys = site.shape[2]
    pq = phys * phys
    group, cuts, batch = 16, 4, 64
    lanes = chi // cuts
    small = phys * width
    table = mpo.transpose(3, 1, 2, 0).reshape(small, small)
    n_sems = 80
    any_spec = pl.BlockSpec(memory_space=pl.ANY)
    vmem = pl.BlockSpec(memory_space=pltpu.VMEM)
    new_left, product = pl.pallas_call(
        functools.partial(kernel, (rows, width, phys, chi, group, cuts, batch)),
        out_shape=(
            jax.ShapeDtypeStruct((rows, width, chi), BF16),
            jax.ShapeDtypeStruct((rows, phys, phys, chi), BF16),
        ),
        in_specs=[any_spec] * 5,
        out_specs=(vmem, vmem),
        scratch_shapes=[
            pltpu.VMEM((2, rows, width, chi), BF16),
            pltpu.VMEM((rows, phys, chi), BF16),
            pltpu.VMEM((rows, phys, phys, chi), BF16),
            pltpu.VMEM((small, small), BF16),
            pltpu.VMEM((width, chi, chi), BF16),
            pltpu.VMEM((phys, rows, chi), BF16),
            pltpu.VMEM((cuts, pq // 2, rows, 2 * lanes), BF16),
            pltpu.VMEM((phys, chi, chi), BF16),
            pltpu.VMEM((2, chi, phys * rows), BF16),
            pltpu.VMEM((small * group, small * group), BF16),
            pltpu.VMEM((width * pq, width * pq), BF16),
            pltpu.VMEM((width, 2, phys * rows, chi // 2), BF16),
            pltpu.VMEM((width, chi, chi // 2), BF16),
            pltpu.VMEM((width, 2 * rows, chi // 2), BF16),
            pltpu.VMEM((width, rows, chi // 2), BF16),
            pltpu.VMEM((width, rows, chi // 2), BF16),
            pltpu.VMEM((rows * width, chi), BF16),
            pltpu.VMEM((rows * width, chi), BF16),
            pltpu.VMEM((cuts, pq // 2, chi, 2 * lanes), BF16),
            pltpu.VMEM((pq // 2, batch * width, 2 * lanes), F32),
            pltpu.VMEM((batch * pq, width * lanes), BF16),
            pltpu.VMEM((cuts, rows * pq, lanes), F32),
            pltpu.SemaphoreType.DMA((6,)),
            pltpu.SemaphoreType.DMA((n_sems,)),
            pltpu.SemaphoreType.DMA((n_sems,)),
        ],
        compiler_params=pltpu.CompilerParams(
            collective_id=0, has_side_effects=True, vmem_limit_bytes=62 * 1024 * 1024
        ),
    )(left_env[0], site[0], psi[0], right_env[0], table)
    return new_left[None], product[None]


def shifted(block, axis, distance):
    devices = range(lax.axis_size(axis))
    route = [((i - distance) % len(devices), i) for i in devices]
    return lax.ppermute(block, axis, route)


def shards(left_env, site, psi, right_env, mpo):
    left = left_env[0]
    tensor = site[0]
    rows = tensor.shape[0]
    phys = tensor.shape[1]
    chi = tensor.shape[2]
    width = left.shape[1]
    pair_source = shifted(psi[0], "sec", 1)
    offset = lax.axis_index("bond") * rows
    whole_left, whole_site = (
        lax.all_gather(left, "bond", axis=0, tiled=True),
        lax.all_gather(tensor, "bond", axis=0, tiled=True),
    )
    own_cols = lax.dynamic_slice_in_dim(whole_site, offset, rows, 2)
    first = jnp.dot(
        whole_left.reshape(chi * width, chi),
        own_cols.reshape(chi, phys * rows),
        preferred_element_type=jnp.float32,
    )
    first = first.astype(jnp.bfloat16).reshape(chi, width, phys, rows)
    second = jnp.einsum("pmsb,mnsu->punb", first, mpo, preferred_element_type=jnp.float32).astype(
        jnp.bfloat16
    )
    fresh = lax.dot_general(
        whole_site.reshape(chi * phys, chi),
        second.reshape(chi * phys, width * rows),
        (((0,), (0,)), ((), ())),
        preferred_element_type=jnp.float32,
    )
    fresh = fresh.astype(jnp.bfloat16).reshape(chi, width, rows)
    new_left = lax.all_to_all(fresh, "bond", split_axis=0, concat_axis=2, tiled=True)
    left_source = shifted(new_left, "sec", 1)
    source_flat = left_source.reshape(rows * width, chi)
    pair = pair_source.reshape(rows, phys * phys * chi)
    mixed = jnp.dot(
        source_flat,
        lax.all_gather(pair, "bond", axis=0, tiled=True),
        preferred_element_type=jnp.float32,
    )
    mixed = mixed.astype(jnp.bfloat16).reshape(rows, width * phys * phys, chi)
    two_site = jnp.einsum("mnsu,nkvw->msvuwk", mpo, mpo, preferred_element_type=jnp.float32)
    two_site = two_site.astype(jnp.bfloat16).reshape(width * phys * phys, phys * phys * width)
    projected = jnp.einsum(
        "pqc,qr->prc", mixed, two_site, preferred_element_type=jnp.float32
    ).astype(jnp.bfloat16)
    env_right = right_env[0].reshape(width * chi, chi)
    result = jnp.dot(
        projected.reshape(rows * phys * phys, width * chi),
        env_right,
        preferred_element_type=jnp.float32,
    ).astype(jnp.bfloat16)
    return (new_left[None], result.reshape(1, rows, phys, phys, chi))


def solution(mesh):
    in_specs = (
        P("sec", "bond", None, None),
        P("sec", "bond", None, None),
        P("sec", "bond", None, None, None),
        P("sec", None, None, None),
        P(),
    )
    out_specs = (P("sec", "bond", None, None), P("sec", "bond", None, None, None))
    body = fused if mesh.shape["bond"] == 4 else shards
    return jax.shard_map(body, mesh=mesh, in_specs=in_specs, out_specs=out_specs, check_vma=False)
```

```python
import functools

import jax
import jax.numpy as jnp
from jax import lax
from jax.experimental import pallas as pl
from jax.experimental.pallas import tpu as pltpu
from jax.sharding import PartitionSpec as P

MESH = pl.DeviceIdType.MESH
BF16 = jnp.bfloat16
F32 = jnp.float32


def mm(a, b):
    return jnp.dot(a, b, preferred_element_type=F32)


def kernel(
    dims,
    left_h, site_h, psi_h, right_h, mpo_h,
    new_left, product,
    left, site_raw, psi_raw, mpo, right,
    site_own, psi_own, site, site_tr, mix, pair,
    second, part, rs1, send2, rs2, nl_own, nl_in, psi, mixed, proj, acc,
    local_sem, send_sem, recv_sem,
):
    rows, width, phys, chi, group, cuts, batch = dims
    n_bond = 4
    pq = phys * phys
    sec = lax.axis_index("sec")
    me = lax.axis_index("bond")
    n_sec = lax.axis_size("sec")
    next_sec = lax.rem(sec + 1, n_sec)
    prev_sec = lax.rem(sec + n_sec - 1, n_sec)
    bx = (me // 2) * 2 + 1 - lax.rem(me, 2)
    by = lax.rem(me + 2, n_bond)
    bd = lax.rem(bx + 2, n_bond)
    x, y = lax.rem(me, 2), me // 2
    to_x = {"bond": bx}
    to_y = {"bond": by}
    to_next = {"sec": next_sec}

    def block(owner):
        return pl.ds(pl.multiple_of(owner * rows, rows), rows)

    loads = {}
    for i, (name, src, dst) in enumerate((
        ("site", site_h, site_raw),
        ("psi", psi_h, psi_raw),
        ("mpo", mpo_h, mpo),
        ("left", left_h, left.at[x]),
        ("right", right_h, right),
    )):
        loads[name] = pltpu.make_async_copy(src, dst, local_sem.at[i])
        loads[name].start()

    barrier = pltpu.get_barrier_semaphore()
    for target in (to_x, to_y, to_next, {"sec": prev_sec}):
        pl.semaphore_signal(barrier, inc=1, device_id=target, device_id_type=MESH)
    pl.semaphore_wait(barrier, 4)

    started = []
    counter = {}

    def slot(key):
        return counter.setdefault(key, len(counter))

    def send(key, src, dst, target):
        i = slot(key)
        copy = pltpu.make_async_remote_copy(
            src_ref=src, dst_ref=dst, send_sem=send_sem.at[i], recv_sem=recv_sem.at[i],
            device_id=target, device_id_type=MESH,
        )
        copy.start()
        started.append(copy)

    def arrive(key, dst, target):
        i = slot(key)
        pltpu.make_async_remote_copy(
            src_ref=dst, dst_ref=dst, send_sem=send_sem.at[i], recv_sem=recv_sem.at[i],
            device_id=target, device_id_type=MESH,
        ).wait_recv()

    lanes = chi // cuts

    loads["site"].wait()
    flat = site_raw[...].astype(F32).reshape(rows * phys, chi)
    for i in range(cuts):
        acc[i, :rows * phys, :] = flat[:, i * lanes:(i + 1) * lanes]
    for t in range(phys):
        for i in range(cuts):
            tile = acc[i, pl.ds(t, rows, stride=phys), :]
            site_own[t, :, i * lanes:(i + 1) * lanes] = tile.astype(BF16)
            site_tr[x, i * lanes:(i + 1) * lanes, t * rows:(t + 1) * rows] = tile.T.astype(BF16)
    site_here = pltpu.make_async_copy(site_own, site.at[:, block(me), :], local_sem.at[5])
    site_here.start()
    send("site_x", site_own, site.at[:, block(me), :], to_x)
    send("left_x", left_h, left.at[x], to_x)

    loads["psi"].wait()
    tall = 8

    @pl.loop(0, rows // tall)
    def _(g):
        flat = psi_raw[pl.ds(pl.multiple_of(g * tall, tall), tall)].astype(F32)
        flat = flat.reshape(tall * pq, chi)
        where = pl.ds(pl.multiple_of(g * tall * pq, tall * pq), tall * pq)
        for i in range(cuts):
            acc[i, where, :] = flat[:, i * lanes:(i + 1) * lanes]

    halves = (pl.ds(0, 5 * pq // 16), pl.ds(5 * pq // 16, pq // 2 - 5 * pq // 16))

    def region(q, owner, sub=None):
        if sub is None:
            return psi.at[q, :, block(owner), :]
        return psi.at[q, halves[sub], block(owner), :]

    for q in range(cuts):
        for t in range(pq):
            at = (t % 2) * lanes
            tile = acc[q, pl.ds(t, rows, stride=pq), :]
            psi_own[q, t // 2, :, at:at + lanes] = tile.astype(BF16)
        if q > 0:
            send(("shift", q - 1), psi_own.at[q - 1], region(q - 1, me), to_next)
    send(("shift", cuts - 1), psi_own.at[cuts - 1], region(cuts - 1, me), to_next)

    def spread(q):
        spread_x(q)
        spread_y(q)

    def spread_x(q):
        arrive(("shift", q), region(q, me), to_next)
        send(("psi_x", q), region(q, me), region(q, me), to_x)

    def spread_y(q):
        send(("psi_y", q), region(q, me), region(q, me), to_y)

    def relay(q):
        relay_y(q)
        relay_x(q)

    def relay_y(q):
        arrive(("psi_x", q), region(q, bx), to_x)
        send(("psi_xy", q), region(q, bx, 0), region(q, bx, 0), to_y)

    def relay_x(q):
        arrive(("psi_y", q), region(q, by), to_y)
        send(("psi_yx", q), region(q, by, 1), region(q, by, 1), to_x)

    def complete(q):
        arrive(("psi_xy", q), region(q, bd, 0), to_y)
        arrive(("psi_yx", q), region(q, bd, 1), to_x)

    loads["mpo"].wait()

    def iota(shape, axis):
        return lax.broadcasted_iota(jnp.int32, shape, axis)

    def one_hot(condition):
        return jnp.where(condition, 1.0, 0.0).astype(BF16)

    small = phys * width
    big = small * group
    tall_code = lax.div(iota((big, small), 0), group)
    spread_rows = one_hot(tall_code == iota((big, small), 1))
    col = iota((small, big), 1)
    col_code = lax.div(col, group * width) * width + lax.rem(col, width)
    spread_cols = one_hot(col_code == iota((small, big), 0))
    wide = mm(mm(spread_rows, mpo[...]).astype(BF16), spread_cols)
    same = lax.rem(iota((big, big), 0), group) == lax.rem(lax.div(iota((big, big), 1), width), group)
    mix[...] = jnp.where(same, wide, 0.0).astype(BF16)

    side = width * pq
    col = iota((small, side), 1)
    col_m = lax.rem(col, width)
    col_sv = lax.rem(lax.div(col, width), pq // 2) * 2 + lax.div(col, width * (pq // 2))
    col_s, col_v = lax.div(col_sv, phys), lax.rem(col_sv, phys)
    row = iota((side, small), 0)
    row_k, row_u, row_w = lax.div(row, pq), lax.rem(lax.div(row, phys), phys), lax.rem(row, phys)
    code_c, code_r = iota((small, side), 0), iota((side, small), 1)
    t1 = mm(mpo[...], one_hot(col_s * width + col_m == code_c)).astype(BF16)
    t2 = mm(one_hot(row_w * width + row_k == code_r), mpo[...]).astype(BF16)
    both = jnp.zeros((side, side), F32)
    for n in range(width):
        near = mm(one_hot(row_u * width + n == code_r), t1)
        both += near * mm(t2, one_hot(col_v * width + n == code_c))
    pair[...] = both.astype(BF16)

    wide_b = chi // 2
    cols = pl.ds(pl.multiple_of(x * wide_b, wide_b), wide_b)

    def pair_rows(which):
        return pl.ds(pl.multiple_of(which * 2 * rows, 2 * rows), 2 * rows)

    site_here.wait()
    arrive("site_x", site.at[:, block(bx), :], to_x)
    ours = site.at[:, pair_rows(y), cols]
    send("site_pair", ours, ours, to_y)
    for t in range(phys):
        for i in range(cuts):
            tile = site[t, block(bx), i * lanes:(i + 1) * lanes].astype(F32)
            place = (slice(i * lanes, (i + 1) * lanes), slice(t * rows, (t + 1) * rows))
            site_tr[(1 - x,) + place] = tile.T.astype(BF16)
    spread(0)
    loads["left"].wait()
    arrive("site_pair", site.at[:, pair_rows(1 - y), cols], to_y)

    strip = group * width

    def fill(which):
        @pl.loop(0, rows // group)
        def _(g):
            ours = left[which, pl.ds(pl.multiple_of(g * group, group), group)].astype(F32)
            ours = ours.reshape(strip, chi).astype(BF16)
            first = [mm(ours, site[t, :, cols]).astype(BF16) for t in range(phys)]
            out = mm(mix[...], jnp.concatenate(first, axis=0)).astype(BF16)
            for u in range(phys):
                for n in range(width):
                    at = (u * width + n) * group
                    where = pl.multiple_of(u * rows + g * group, group)
                    second[n, which, pl.ds(where, group), :] = out[at:at + group, :]

    fill(x)
    arrive("left_x", left.at[1 - x], to_x)
    fill(1 - x)

    def first_round(n):
        send(("rs", n), part.at[n, pair_rows(1 - y), :], rs1.at[n], to_y)

    def second_round(n):
        send(("swap", n), send2.at[n], rs2.at[n], to_x)

    for n in range(width):
        part[n] = (mm(site_tr[0], second[n, 0]) + mm(site_tr[1], second[n, 1])).astype(BF16)
        if n > 0:
            first_round(n - 1)
    first_round(width - 1)
    relay_x(0)
    spread_x(1)

    def block_in_pair(which):
        return pl.ds(pl.multiple_of(which * rows, rows), rows)

    for n in range(width):
        arrive(("rs", n), rs1.at[n], to_y)
        far = part[n, block(bx), :].astype(F32) + rs1[n, block_in_pair(1 - x), :].astype(F32)
        send2[n] = far.astype(BF16)
        own = part[n, block(me), :].astype(F32) + rs1[n, block_in_pair(x), :].astype(F32)
        for i in range(cuts // 2):
            acc[x * (cuts // 2) + i, pl.ds(n, rows, stride=width), :] = own[:, i * lanes:(i + 1) * lanes]
        if n > 0:
            second_round(n - 1)
    second_round(width - 1)
    relay_y(0)
    spread_y(1)
    for n in range(width):
        arrive(("swap", n), rs2.at[n], to_x)
        other = rs2[n].astype(F32)
        for i in range(cuts // 2):
            at = (1 - x) * (cuts // 2) + i
            acc[at, pl.ds(n, rows, stride=width), :] = other[:, i * lanes:(i + 1) * lanes]
    whole = jnp.concatenate([acc[i, :rows * width, :] for i in range(cuts)], axis=1)
    nl_own[...] = whole.astype(BF16)
    new_left[...] = whole.reshape(rows, width, chi).astype(BF16)
    send("left", nl_own, nl_in, to_next)
    relay(1)
    spread(2)
    loads["right"].wait()
    arrive("left", nl_in, to_next)

    for q in range(cuts):
        complete(q)

        def strip_of(g):
            high = batch * width
            ours = nl_in[pl.ds(pl.multiple_of(g * high, high), high), :]

            @pl.loop(0, pq // 2)
            def _(t):
                mixed[t] = mm(ours, psi[q, t])

            @pl.loop(0, batch // 2, unroll=4)
            def _(p):
                here = mixed[:, pl.ds(pl.multiple_of(p * 2 * width, 2 * width), 2 * width), :]
                tiles = []
                for i in range(2):
                    one = here[:, i * width:(i + 1) * width, :].reshape(pq // 2 * width, 2 * lanes)
                    tiles.append(jnp.concatenate([one[:, :lanes], one[:, lanes:]], axis=0))
                both = jnp.concatenate(tiles, axis=1).astype(BF16)
                out = mm(pair[...], both).astype(BF16)
                for i in range(2):
                    where = pl.ds(pl.multiple_of((p * 2 + i) * pq, pq), pq)
                    for k in range(width):
                        piece = out[k * pq:(k + 1) * pq, i * lanes:(i + 1) * lanes]
                        proj[where, k * lanes:(k + 1) * lanes] = piece

            env = right[:, q * lanes:(q + 1) * lanes, :].reshape(width * lanes, chi)
            total = mm(proj[...], env)
            long = pl.ds(pl.multiple_of(g * batch * pq, batch * pq), batch * pq)
            if q > 0:
                total += jnp.concatenate([acc[i, long, :] for i in range(cuts)], axis=1)
            if q < cuts - 1:
                for i in range(cuts):
                    acc[i, long, :] = total[:, i * lanes:(i + 1) * lanes]
            else:
                out = total.reshape(batch, phys, phys, chi).astype(BF16)
                product[pl.ds(pl.multiple_of(g * batch, batch), batch)] = out

        if 0 < q < cuts - 1:
            strip_of(0)
            relay(q + 1)
            if q + 2 < cuts:
                spread(q + 2)
            pl.loop(1, rows // batch)(strip_of)
        else:
            pl.loop(0, rows // batch)(strip_of)

    for copy in started:
        copy.wait_send()


def fused(left_env, site, psi, right_env, mpo):
    _, rows, width, chi = left_env.shape
    phys = site.shape[2]
    pq = phys * phys
    group, cuts, batch = 16, 4, 64
    lanes = chi // cuts
    small = phys * width
    table = mpo.transpose(3, 1, 2, 0).reshape(small, small)
    n_sems = 80
    any_spec = pl.BlockSpec(memory_space=pl.ANY)
    vmem = pl.BlockSpec(memory_space=pltpu.VMEM)
    new_left, product = pl.pallas_call(
        functools.partial(kernel, (rows, width, phys, chi, group, cuts, batch)),
        out_shape=(
            jax.ShapeDtypeStruct((rows, width, chi), BF16),
            jax.ShapeDtypeStruct((rows, phys, phys, chi), BF16),
        ),
        in_specs=[any_spec] * 5,
        out_specs=(vmem, vmem),
        scratch_shapes=[
            pltpu.VMEM((2, rows, width, chi), BF16),
            pltpu.VMEM((rows, phys, chi), BF16),
            pltpu.VMEM((rows, phys, phys, chi), BF16),
            pltpu.VMEM((small, small), BF16),
            pltpu.VMEM((width, chi, chi), BF16),
            pltpu.VMEM((phys, rows, chi), BF16),
            pltpu.VMEM((cuts, pq // 2, rows, 2 * lanes), BF16),
            pltpu.VMEM((phys, chi, chi), BF16),
            pltpu.VMEM((2, chi, phys * rows), BF16),
            pltpu.VMEM((small * group, small * group), BF16),
            pltpu.VMEM((width * pq, width * pq), BF16),
            pltpu.VMEM((width, 2, phys * rows, chi // 2), BF16),
            pltpu.VMEM((width, chi, chi // 2), BF16),
            pltpu.VMEM((width, 2 * rows, chi // 2), BF16),
            pltpu.VMEM((width, rows, chi // 2), BF16),
            pltpu.VMEM((width, rows, chi // 2), BF16),
            pltpu.VMEM((rows * width, chi), BF16),
            pltpu.VMEM((rows * width, chi), BF16),
            pltpu.VMEM((cuts, pq // 2, chi, 2 * lanes), BF16),
            pltpu.VMEM((pq // 2, batch * width, 2 * lanes), F32),
            pltpu.VMEM((batch * pq, width * lanes), BF16),
            pltpu.VMEM((cuts, rows * pq, lanes), F32),
            pltpu.SemaphoreType.DMA((6,)),
            pltpu.SemaphoreType.DMA((n_sems,)),
            pltpu.SemaphoreType.DMA((n_sems,)),
        ],
        compiler_params=pltpu.CompilerParams(
            collective_id=0, has_side_effects=True, vmem_limit_bytes=62 * 1024 * 1024
        ),
    )(left_env[0], site[0], psi[0], right_env[0], table)
    return new_left[None], product[None]


def shifted(block, axis, distance):
    devices = range(lax.axis_size(axis))
    route = [((i - distance) % len(devices), i) for i in devices]
    return lax.ppermute(block, axis, route)


def shards(left_env, site, psi, right_env, mpo):
    left = left_env[0]
    tensor = site[0]
    rows = tensor.shape[0]
    phys = tensor.shape[1]
    chi = tensor.shape[2]
    width = left.shape[1]
    pair_source = shifted(psi[0], "sec", 1)
    offset = lax.axis_index("bond") * rows
    whole_left, whole_site = (
        lax.all_gather(left, "bond", axis=0, tiled=True),
        lax.all_gather(tensor, "bond", axis=0, tiled=True),
    )
    own_cols = lax.dynamic_slice_in_dim(whole_site, offset, rows, 2)
    first = jnp.dot(
        whole_left.reshape(chi * width, chi),
        own_cols.reshape(chi, phys * rows),
        preferred_element_type=jnp.float32,
    )
    first = first.astype(jnp.bfloat16).reshape(chi, width, phys, rows)
    second = jnp.einsum("pmsb,mnsu->punb", first, mpo, preferred_element_type=jnp.float32).astype(
        jnp.bfloat16
    )
    fresh = lax.dot_general(
        whole_site.reshape(chi * phys, chi),
        second.reshape(chi * phys, width * rows),
        (((0,), (0,)), ((), ())),
        preferred_element_type=jnp.float32,
    )
    fresh = fresh.astype(jnp.bfloat16).reshape(chi, width, rows)
    new_left = lax.all_to_all(fresh, "bond", split_axis=0, concat_axis=2, tiled=True)
    left_source = shifted(new_left, "sec", 1)
    source_flat = left_source.reshape(rows * width, chi)
    pair = pair_source.reshape(rows, phys * phys * chi)
    mixed = jnp.dot(
        source_flat,
        lax.all_gather(pair, "bond", axis=0, tiled=True),
        preferred_element_type=jnp.float32,
    )
    mixed = mixed.astype(jnp.bfloat16).reshape(rows, width * phys * phys, chi)
    two_site = jnp.einsum("mnsu,nkvw->msvuwk", mpo, mpo, preferred_element_type=jnp.float32)
    two_site = two_site.astype(jnp.bfloat16).reshape(width * phys * phys, phys * phys * width)
    projected = jnp.einsum(
        "pqc,qr->prc", mixed, two_site, preferred_element_type=jnp.float32
    ).astype(jnp.bfloat16)
    env_right = right_env[0].reshape(width * chi, chi)
    result = jnp.dot(
        projected.reshape(rows * phys * phys, width * chi),
        env_right,
        preferred_element_type=jnp.float32,
    ).astype(jnp.bfloat16)
    return (new_left[None], result.reshape(1, rows, phys, phys, chi))


def solution(mesh):
    in_specs = (
        P("sec", "bond", None, None),
        P("sec", "bond", None, None),
        P("sec", "bond", None, None, None),
        P("sec", None, None, None),
        P(),
    )
    out_specs = (P("sec", "bond", None, None), P("sec", "bond", None, None, None))
    body = fused if mesh.shape["bond"] == 4 else shards
    return jax.shard_map(body, mesh=mesh, in_specs=in_specs, out_specs=out_specs, check_vma=False)
```
